32 devices in a mesh: row: 4 (over z), col: 8 (over y, x, core).
Axes of the slice: x: 2, y: 2, z: 4, core: 2. Of those that a mesh axis runs over, the one named last changes fastest.
Arguments:
- covariance: float32 [16384, 16384], P('row', 'col'), may hold values from -1 to 3, as said below
- center: float32 [16384], replicated, may hold values from 0.4 to 1
- links: float32 [4, 16384], replicated, may hold values from 0.05 to 0.25
- process: float32 [16384], replicated, may hold values from 0.1 to 1
- wells: int32 [1, 256], replicated, may hold values from 0 to 16383, as said below
- noise: float32 [1, 256], replicated, may hold values from 0.05 to 0.5
Outputs:
- updated: float32 [16384, 16384], P('row', 'col')
The draws below stay inside these ranges and needn't reach their ends.
Inputs may be any that keep to these rules, and one draw needn't show every extreme that they name: `covariance`: symmetric positive definite. `wells`: each row holds 256 distinct cells; at most 32 of them lie in one aligned block of 2048 cells, and exactly 32 in some block.
All inputs are finite; a program needn't handle non-finite values.
Results may differ from the reference program's by a relative error of at most 0.0001.
Values sent between devices are 32-bit elements; how exact they have to be, the bound alone decides.
A program may use at most 320 MiB of HBM per device.

```python
import math
import jax
import jax.numpy as jnp
from jax import lax

NGX = 128
NGY = 128
M = 256
WMAX = 32
STEPS = 1
NCELL = 16384
CBLK = 2048


def draw_covariance(key, part):
    base = jax.random.normal(key, (NCELL, NCELL), jnp.float32)
    lift = 2.0
    sym = (base + base.T) * (0.5 / math.sqrt(NCELL))
    return sym + lift * jnp.eye(NCELL, dtype=jnp.float32)


def draw_wells(key, part):
    blocks = NCELL // CBLK
    keys = jax.random.split(jax.random.fold_in(key, 11), STEPS * blocks)
    perms = jax.vmap(lambda k: jax.random.permutation(k, CBLK))(keys).reshape(STEPS, blocks, CBLK)
    first = jax.random.randint(jax.random.fold_in(key, 12), (STEPS,), 0, blocks)
    slot = jnp.arange(M, dtype=jnp.int32)
    later = jnp.maximum(slot - WMAX, 0)
    span = max(blocks - 1, 1)
    block = jnp.where(slot[None, :] < WMAX, first[:, None], (first[:, None] + 1 + later[None, :] % span) % blocks)
    rank = jnp.where(slot[None, :] < WMAX, slot[None, :], later[None, :] // span)
    offset = perms[jnp.arange(STEPS, dtype=jnp.int32)[:, None], block, rank]
    cells = (block * CBLK + offset).astype(jnp.int32)
    orders = jax.vmap(lambda k: jax.random.permutation(k, M))(jax.random.split(jax.random.fold_in(key, 13), STEPS))
    return jnp.take_along_axis(cells, orders.astype(jnp.int32), axis=1).astype(jnp.int32)


def setup_inputs(seed: int = 0) -> dict:
    arg_keys = jax.random.split(jax.random.key(seed), 7)
    covariance = draw_covariance(jax.random.fold_in(arg_keys[6], 71), 0)
    center = jnp.clip(jnp.exp(jax.random.uniform(arg_keys[1], (NCELL,), jnp.float32, math.log(0.4), math.log(1.0))), 0.4, 1.0)
    links = jnp.clip(jnp.exp(jax.random.uniform(arg_keys[2], (4, NCELL), jnp.float32, math.log(0.05), math.log(0.25))), 0.05, 0.25)
    process = jnp.clip(jnp.exp(jax.random.uniform(arg_keys[3], (NCELL,), jnp.float32, math.log(0.1), math.log(1.0))), 0.1, 1.0)
    wells = draw_wells(jax.random.fold_in(arg_keys[6], 71), 0)
    noise = jnp.clip(jnp.exp(jax.random.uniform(arg_keys[5], (STEPS, M), jnp.float32, math.log(0.05), math.log(0.5))), 0.05, 0.5)
    return dict(covariance=covariance, center=center, links=links, process=process, wells=wells, noise=noise)


def apply_left(matrix, center, links):
    field = matrix.reshape(NGX, NGY, -1)
    padded = jnp.pad(field, ((1, 1), (1, 1), (0, 0)))
    own = center.reshape(NGX, NGY, 1)
    coef = links.reshape(4, NGX, NGY, 1)
    out = own * field + coef[0] * padded[:-2, 1:-1] + coef[1] * padded[2:, 1:-1]
    out = out + coef[2] * padded[1:-1, :-2] + coef[3] * padded[1:-1, 2:]
    return out.reshape(NCELL, -1)

def apply_right(matrix, center, links):
    field = matrix.reshape(-1, NGX, NGY)
    padded = jnp.pad(field, ((0, 0), (1, 1), (1, 1)))
    own = center.reshape(1, NGX, NGY)
    coef = links.reshape(4, 1, NGX, NGY)
    out = own * field + coef[0] * padded[:, :-2, 1:-1] + coef[1] * padded[:, 2:, 1:-1]
    out = out + coef[2] * padded[:, 1:-1, :-2] + coef[3] * padded[:, 1:-1, 2:]
    return out.reshape(-1, NCELL)

def reference(covariance, center, links, process, wells, noise):
    current = covariance
    diag_index = jnp.arange(NCELL, dtype=jnp.int32)
    for step in range(STEPS):
        left = apply_left(current, center, links)
        predicted = apply_right(left, center, links)
        predicted = predicted.at[diag_index, diag_index].add(process)
        chosen = wells[step]
        strip = jnp.take(predicted, chosen, axis=1)
        across = jnp.take(predicted, chosen, axis=0)
        innovation = jnp.take(strip, chosen, axis=0) + jnp.diag(noise[step])
        factor = jnp.linalg.cholesky(innovation)
        solved = jax.scipy.linalg.cho_solve((factor, True), across)
        current = predicted - jnp.dot(strip, solved, precision=lax.Precision.HIGHEST)
    return current
```

```python
import functools

import jax
import jax.numpy as jnp
from jax import lax
from jax.experimental import pallas as pl
from jax.experimental.pallas import tpu as pltpu
from jax.sharding import PartitionSpec as P

NGY = 128
WMAX = 32
PANEL = 32
PAD = 8
HIGHEST = lax.Precision.HIGHEST
F32 = jnp.float32
BF16 = jnp.bfloat16
MESH = pl.DeviceIdType.MESH


def iota(shape, dim):
    return lax.broadcasted_iota(jnp.int32, shape, dim).astype(F32)


def rowdot(a, b, precision=HIGHEST):
    return lax.dot_general(
        a, b, (((1,), (1,)), ((), ())), precision=precision, preferred_element_type=F32
    )


def coldot(a, b, precision=HIGHEST):
    return lax.dot_general(
        a, b, (((0,), (0,)), ((), ())), precision=precision, preferred_element_type=F32
    )


def prep_kernel(
    nrow, wells_ref, noise_ref, center_ref, links_ref, process_ref, cov_ref,
    bp_ref, sp_ref, ownc_ref, ownp_ref, colc_ref, diag_ref,
    tables, cells, rows_v, rows_s, coef, near, spill, idx_sem, near_sem, spill_sem,
):
    rows, cols = cov_ref.shape
    m = wells_ref.shape[1]
    slots = diag_ref.shape[0]
    ngx = center_ref.shape[0]
    own = bp_ref.shape[0]
    span = own + 2 * WMAX
    r = lax.axis_index("row")
    c = lax.axis_index("col")

    w = wells_ref[...].astype(F32)
    block = jnp.floor(w * (1.0 / cols))
    square = jnp.broadcast_to(block, (m, m)).T
    earlier = (square == block) & (iota((m, m), 0) < iota((m, m), 1))
    rank = jnp.sum(jnp.where(earlier, 1.0, 0.0), axis=0, keepdims=True)
    slot = block * WMAX + rank
    onehot = slot == iota((slots, m), 0)
    cell = jnp.sum(jnp.where(onehot, w + 1.0, 0.0), axis=1, keepdims=True) - 1.0
    noise = jnp.sum(jnp.where(onehot, noise_ref[...], 0.0), axis=1, keepdims=True)
    diag_ref[...] = jnp.broadcast_to(jnp.where(cell < 0.0, 1.0, noise), diag_ref.shape)
    cells[...] = jnp.full(cells.shape, -1.0, F32)
    cells[WMAX : WMAX + slots, :] = jnp.broadcast_to(cell, (slots, NGY))

    mine = cells[pl.ds(pl.multiple_of(r * own, WMAX), span), :]
    colc_ref[...] = cells[pl.ds(pl.multiple_of(WMAX + c * WMAX, WMAX), WMAX), :]
    ownc_ref[...] = mine[WMAX : WMAX + own]
    local = mine - (r * rows).astype(F32)
    rows_v[...] = local.T[0:8].astype(jnp.int32)
    copy = pltpu.make_async_copy(rows_v, rows_s, idx_sem)
    copy.start()

    for t in range(6):
        if t == 0:
            tables[:, :NGY] = center_ref[...]
        elif t < 5:
            tables[:, t * NGY : (t + 1) * NGY] = links_ref[(t - 1) * ngx : t * ngx, :]
        else:
            tables[:, t * NGY : (t + 1) * NGY] = process_ref[...]
    gx = jnp.floor(mine[:, :1] * (1.0 / NGY))
    gy = mine[:, :1] - gx * NGY
    pickx = jnp.where(gx == iota((span, ngx), 1), 1.0, 0.0)
    table = jnp.dot(pickx, tables[...], precision=HIGHEST)
    copy.wait()

    moves = (0, -NGY, NGY, -1, 1)

    def row(i):
        return cov_ref.at[pl.ds(jnp.clip(i, 0, rows - 1), 1), :]

    def gather(i, carry):
        at = rows_s[0, WMAX + i]
        for t in range(5):
            dst = near.at[pl.ds(t * own + i, 1), :]
            pltpu.make_async_copy(row(at + moves[t]), dst, near_sem).start()
        return carry

    lax.fori_loop(0, own, gather, 0)

    def gather_spill(i, carry):
        low = spill.at[pl.ds(i, 1), :]
        high = spill.at[pl.ds(WMAX + i, 1), :]
        pltpu.make_async_copy(row(rows_s[0, i] + NGY), low, spill_sem).start()
        pltpu.make_async_copy(row(rows_s[0, WMAX + own + i] - NGY), high, spill_sem).start()
        return carry

    lax.fori_loop(0, WMAX, gather_spill, 0)

    picky = gy == iota((span, NGY), 1)
    valid = mine[:, :1] >= 0.0
    lv = local[:, :1]
    for t in range(5):
        value = jnp.sum(
            jnp.where(picky, table[:, t * NGY : (t + 1) * NGY], 0.0), axis=1, keepdims=True
        )
        target = lv + moves[t]
        ok = valid & (target >= 0.0) & (target < rows)
        if t == 3:
            ok = ok & (gy > 0.0)
        if t == 4:
            ok = ok & (gy < NGY - 1.0)
        coef[t] = jnp.broadcast_to(jnp.where(ok, value, 0.0), (span, NGY))
    value = jnp.sum(jnp.where(picky, table[:, 5 * NGY :], 0.0), axis=1, keepdims=True)
    value = jnp.where(valid, value, 0.0)
    ownp_ref[...] = jnp.broadcast_to(value[WMAX : WMAX + own], (own, NGY))

    pltpu.make_async_copy(cov_ref.at[pl.ds(0, 5 * own), :], near, near_sem).wait()
    pltpu.make_async_copy(cov_ref.at[pl.ds(0, 2 * WMAX), :], spill, spill_sem).wait()
    for k in range(cols // NGY):
        at = slice(k * NGY, (k + 1) * NGY)
        acc = coef[0, WMAX : WMAX + own] * near[0:own, at]
        for t in range(1, 5):
            acc = acc + coef[t, WMAX : WMAX + own] * near[t * own : (t + 1) * own, at]
        bp_ref[:, at] = acc
        sp_ref[:WMAX, at] = coef[2, :WMAX] * spill[:WMAX, at]
        sp_ref[WMAX:, at] = coef[1, WMAX + own :] * spill[WMAX:, at]


def prep(nrow, ncol, wells, noise, center, links, process, cov):
    rows, cols = cov.shape
    ratio = rows // cols
    own = ratio * WMAX
    slots = ncol * WMAX
    span = own + 2 * WMAX
    m = wells.shape[1]
    vmem = pl.BlockSpec(memory_space=pltpu.VMEM)
    out = lambda *s: jax.ShapeDtypeStruct(s, F32)
    return pl.pallas_call(
        functools.partial(prep_kernel, nrow),
        in_specs=[vmem] * 5 + [pl.BlockSpec(memory_space=pl.ANY)],
        out_specs=[vmem] * 6,
        out_shape=[
            out(own, cols), out(2 * WMAX, cols), out(own, NGY), out(own, NGY),
            out(WMAX, NGY), out(slots, NGY),
        ],
        scratch_shapes=[
            pltpu.VMEM((center.shape[0], 6 * NGY), F32),
            pltpu.VMEM((slots + 2 * WMAX, NGY), F32),
            pltpu.VMEM((8, span), jnp.int32),
            pltpu.SMEM((8, span), jnp.int32),
            pltpu.VMEM((5, span, NGY), F32),
            pltpu.VMEM((5 * own, cols), F32),
            pltpu.VMEM((2 * WMAX, cols), F32),
            pltpu.SemaphoreType.DMA,
            pltpu.SemaphoreType.DMA,
            pltpu.SemaphoreType.DMA,
        ],
        compiler_params=pltpu.CompilerParams(vmem_limit_bytes=24 * 2**20),
        name="prep",
    )(wells, noise, center, links, process, cov)


def main_kernel(
    nrow, ncol,
    cov_ref, bp_ref, sp_ref, ownc_ref, ownp_ref, colc_ref, diag_ref,
    center_ref, links_ref, process_ref,
    pred_ref, w_ref, strip_ref,
    ccol, cb, xbuf, ring, lh, rh, rtop, rbot, rfirst,
    spin, hl, hr, across, gz, smat, tmat, dcol,
    x_sem, col_send, col_recv, spin_send, spin_recv, edge_send, edge_recv,
    gz_send, gz_recv, s_send, s_recv, ac_send, ac_recv, halo_send, halo_recv,
    ring_send, ring_recv, swap_send, swap_recv,
):
    rows, cols = cov_ref.shape
    rt = rows // NGY
    ct = cols // NGY
    own = bp_ref.shape[0]
    half = own // 2
    slots = across.shape[0]
    ngx = center_ref.shape[0]
    r = lax.axis_index("row")
    c = lax.axis_index("col")
    up, down = r > 0, r < nrow - 1
    lef, rig = c > 0, c < ncol - 1
    one = lambda cond: jnp.where(cond, 1, 0)

    def remote(src, dst, ssem, rsem, dr, dc):
        return pltpu.make_async_remote_copy(
            src_ref=src, dst_ref=dst, send_sem=ssem, recv_sem=rsem,
            device_id={"row": dr, "col": dc}, device_id_type=MESH,
        )

    base = pl.multiple_of(c * ct, 8)
    lane = lax.broadcasted_iota(jnp.int32, (ct, NGY), 1)
    ccol[0] = center_ref[pl.ds(base, ct), :]
    for t in range(4):
        v = links_ref[pl.ds(pl.multiple_of(t * ngx + base, 8), ct), :]
        if t == 2:
            v = jnp.where(lane == 0, 0.0, v)
        if t == 3:
            v = jnp.where(lane == NGY - 1, 0.0, v)
        ccol[t + 1] = v

    ring[...] = jnp.zeros(ring.shape, F32)

    @pl.when(r == 0)
    def _():
        rtop[...] = jnp.zeros(rtop.shape, F32)
        spin[0] = jnp.zeros(spin.shape[1:], F32)
        hl[1] = jnp.zeros(hl.shape[1:], F32)
        hr[1] = jnp.zeros(hr.shape[1:], F32)

    @pl.when(r == nrow - 1)
    def _():
        rbot[...] = jnp.zeros(rbot.shape, F32)
        spin[1] = jnp.zeros(spin.shape[1:], F32)
        hl[2] = jnp.zeros(hl.shape[1:], F32)
        hr[2] = jnp.zeros(hr.shape[1:], F32)

    @pl.when(c == 0)
    def _():
        lh[...] = jnp.zeros(lh.shape, F32)
        hl[...] = jnp.zeros(hl.shape, F32)

    @pl.when(c == ncol - 1)
    def _():
        rh[...] = jnp.zeros(rh.shape, F32)
        hr[...] = jnp.zeros(hr.shape, F32)

    bar = pltpu.get_barrier_semaphore()

    def greet(dr, dc):
        pl.semaphore_signal(bar, 1, device_id={"row": dr, "col": dc}, device_id_type=MESH)

    for d in range(1, nrow):
        greet(lax.rem(r + d, nrow), c)
    for d in range(1, ncol):
        greet(r, lax.rem(c + d, ncol))
    for dr, okr in ((-1, up), (1, down)):
        for dc, okc in ((-1, lef), (1, rig)):
            @pl.when(okr & okc)
            def _():
                greet(r + dr, c + dc)
    diagonals = (one(up) + one(down)) * (one(lef) + one(rig))
    pl.semaphore_wait(bar, nrow - 1 + ncol - 1 + diagonals)

    half_rows = lambda k: pl.ds(k * WMAX, WMAX)
    small = []

    def exchange(cond_send, cond_recv, src, dst, ssem, rsem, dr, dc):
        copy = remote(src, dst, ssem, rsem, dr, dc)
        pl.when(cond_send)(copy.start)
        small.append((cond_send, cond_recv, copy))

    exchange(up, down, sp_ref.at[half_rows(0)], spin.at[1], spin_send.at[0], spin_recv.at[0], r - 1, c)
    exchange(down, up, sp_ref.at[half_rows(1)], spin.at[0], spin_send.at[1], spin_recv.at[1], r + 1, c)
    for side, ok, no, buf, dc in ((0, lef, rig, hr, -1), (1, rig, lef, hl, 1)):
        at = slice(0, NGY) if side == 0 else slice(cols - NGY, cols)
        exchange(ok, no, bp_ref.at[:, at], buf.at[0], edge_send.at[side, 0], edge_recv.at[side, 0], r, c + dc)
        exchange(
            up & ok, down & no, sp_ref.at[half_rows(0), at], buf.at[2, half_rows(0)],
            edge_send.at[side, 1], edge_recv.at[side, 1], r - 1, c + dc,
        )
        exchange(
            down & ok, up & no, sp_ref.at[half_rows(1), at], buf.at[1, half_rows(0)],
            edge_send.at[side, 2], edge_recv.at[side, 2], r + 1, c + dc,
        )

    nchunk = col_send.shape[1]
    crows = rows // nchunk
    cols_out = []
    for n in range(nchunk):
        at = pl.ds(n * crows, crows)
        to_left = remote(cov_ref.at[at, 0:NGY], rh.at[at], col_send.at[0, n], col_recv.at[0, n], r, c - 1)
        to_right = remote(
            cov_ref.at[at, cols - NGY : cols], lh.at[at], col_send.at[1, n], col_recv.at[1, n], r, c + 1
        )
        pl.when(lef)(to_left.start)
        pl.when(rig)(to_right.start)
        cols_out.append((to_left, to_right))

    def fetch(t):
        b = lax.rem(t, 3)
        return pltpu.make_async_copy(
            cov_ref.at[pl.ds(pl.multiple_of(t * NGY, NGY), NGY), :], xbuf.at[b], x_sem.at[b]
        )

    fetch(0).start()
    fetch(1).start()

    for cond_send, cond_recv, copy in small:
        pl.when(cond_recv)(copy.wait_recv)

    mine = pl.ds(pl.multiple_of(r * own, own), own)

    def total(k):
        if k < 0:
            main, top, bottom = hl[0], hl[1, 0:WMAX], hl[2, 0:WMAX]
        elif k == ct:
            main, top, bottom = hr[0], hr[1, 0:WMAX], hr[2, 0:WMAX]
        else:
            at = slice(k * NGY, (k + 1) * NGY)
            main, top, bottom = bp_ref[:, at], spin[0, :, at], spin[1, :, at]
        if own == 2 * WMAX:
            return main + jnp.concatenate([top, bottom], axis=0)
        gap = jnp.zeros((own - 2 * WMAX, NGY), F32)
        return main + jnp.concatenate([top, gap, bottom], axis=0)

    cell_at = ownc_ref[...] - (c * cols).astype(F32)
    before, here = total(-1), total(0)
    for k in range(ct):
        after = total(k + 1)
        acc = ccol[0, k : k + 1] * here + ccol[1, k : k + 1] * before + ccol[2, k : k + 1] * after
        acc = acc + ccol[3, k : k + 1] * pltpu.roll(here, 1, 1)
        acc = acc + ccol[4, k : k + 1] * pltpu.roll(here, NGY - 1, 1)
        hit = cell_at == iota((own, NGY), 1) + k * NGY
        acc = acc + jnp.where(hit, ownp_ref[...], 0.0)
        across[mine, k * NGY : (k + 1) * NGY] = acc
        before, here = here, after

    pick_at = colc_ref[...] - (c * cols).astype(F32)
    gram = jnp.zeros((WMAX, own), F32)
    for k in range(ct):
        pick = jnp.where(pick_at == iota((WMAX, NGY), 1) + k * NGY, 1.0, 0.0)
        gram = gram + rowdot(pick, across[mine, k * NGY : (k + 1) * NGY])
    gz[r, :, 0:own] = gram

    gz_out, ac_out = [], []
    for d in range(1, nrow):
        peer = lax.rem(r + d, nrow)
        copy = remote(gz.at[r], gz.at[r], gz_send.at[d - 1], gz_recv.at[r], peer, c)
        copy.start()
        gz_out.append(copy)
    for d in range(1, nrow):
        peer = lax.rem(r + d, nrow)
        copy = remote(across.at[mine], across.at[mine], ac_send.at[d - 1], ac_recv.at[r], peer, c)
        copy.start()
        ac_out.append(copy)
    for d in range(1, nrow):
        src = lax.rem(r + d, nrow)
        remote(gz.at[src], gz.at[src], gz_send.at[0], gz_recv.at[src], src, c).wait_recv()
    srow = pl.ds(pl.multiple_of(c * WMAX, WMAX), WMAX)
    for j in range(nrow):
        smat[srow, j * own : (j + 1) * own] = gz[j, :, 0:own]
    s_out = []
    for d in range(1, ncol):
        peer = lax.rem(c + d, ncol)
        copy = remote(smat.at[srow], smat.at[srow], s_send.at[d - 1], s_recv.at[c], r, peer)
        copy.start()
        s_out.append(copy)
    for d in range(1, ncol):
        src = lax.rem(c + d, ncol)
        at = pl.ds(pl.multiple_of(src * WMAX, WMAX), WMAX)
        remote(smat.at[at], smat.at[at], s_send.at[0], s_recv.at[src], r, src).wait_recv()

    eye = iota((slots, slots), 0) == iota((slots, slots), 1)
    for k in range(slots // NGY):
        at = slice(k * NGY, (k + 1) * NGY)
        tmat[:, at] = smat[:, at] + jnp.where(eye[:, at], diag_ref[...], 0.0)
    tmat[:, slots:] = jnp.where(eye, 1.0, 0.0)
    lanes = lax.broadcasted_iota(jnp.int32, (PANEL, NGY), 1)
    subs = lax.broadcasted_iota(jnp.int32, (PANEL, NGY), 0)

    def panel(p, carry):
        at = pl.ds(pl.multiple_of(p * PANEL, PANEL), PANEL)
        per = NGY // PANEL
        block = tmat[at, 0:NGY]
        for t in range(1, slots // NGY):
            block = jnp.where(p // per == t, tmat[at, t * NGY : (t + 1) * NGY], block)
        block = pltpu.roll(block, lax.rem(per - lax.rem(p, per), per) * PANEL, 1)
        a = jnp.where(lanes < PANEL, block, jnp.where(lanes - PANEL == subs, 1.0, 0.0))
        for k in range(PANEL - 1):
            row = a[k : k + 1, :]
            col = jnp.where(subs > k, jnp.broadcast_to(a[:, k : k + 1], (PANEL, NGY)), 0.0)
            pivot = jnp.broadcast_to(row[:, k : k + 1], (1, NGY))
            a = a - col * (row / pivot)
        pivots = jnp.sum(jnp.where(lanes == subs, a, 0.0), axis=1, keepdims=True)
        dinv = jnp.broadcast_to(1.0 / pivots, (PANEL, NGY))
        dcol[at, :] = dinv
        low = pltpu.roll(a, NGY - PANEL, 1)[:, 0:PANEL]
        u = jnp.dot(low, tmat[at, :], precision=HIGHEST)
        tmat[at, :] = u
        right = lax.broadcasted_iota(jnp.int32, (PANEL, slots), 1) >= (p + 1) * PANEL
        x = jnp.where(right, u[:, 0:slots] * dinv[:, 0:1], 0.0)
        tmat[...] = tmat[...] - coldot(x, u)
        return carry

    lax.fori_loop(0, slots // PANEL, panel, 0)

    RG = 16
    groups = NGY // RG

    def right_apply(t, dst):
        b = lax.rem(t, 3)

        def body(g, carry):
            at = pl.ds(pl.multiple_of(g * RG, RG), RG)
            gat = pl.ds(pl.multiple_of(t * NGY + g * RG, RG), RG)
            before, here = lh[gat, :], xbuf[b, at, 0:NGY]
            for k in range(ct):
                after = xbuf[b, at, (k + 1) * NGY : (k + 2) * NGY] if k < ct - 1 else rh[gat, :]
                acc = ccol[0, k : k + 1] * here + ccol[1, k : k + 1] * before
                acc = acc + ccol[2, k : k + 1] * after
                acc = acc + ccol[3, k : k + 1] * pltpu.roll(here, 1, 1)
                acc = acc + ccol[4, k : k + 1] * pltpu.roll(here, NGY - 1, 1)
                dst[k, pl.ds(pl.multiple_of(PAD + g * RG, 8), RG), :] = acc
                before, here = here, after
            return carry

        lax.fori_loop(0, groups, body, 0)

    def row_coefs(i):
        gx = r * rt + i
        sub = lax.broadcasted_iota(jnp.int32, (NGY, NGY), 0)
        for t in range(5):
            v = center_ref[pl.ds(gx, 1), :] if t == 0 else links_ref[pl.ds((t - 1) * ngx + gx, 1), :]
            v = jnp.broadcast_to(v, (NGY, NGY)).T
            if t == 3:
                v = jnp.where(sub == 0, 0.0, v)
            if t == 4:
                v = jnp.where(sub == NGY - 1, 0.0, v)
            cb[t] = v

    def wait_cols(n):
        pl.when(rig)(cols_out[n][0].wait_recv)
        pl.when(lef)(cols_out[n][1].wait_recv)

    for n in range(nchunk):
        wait_cols(n)
    fetch(0).wait()
    fetch(2).start()
    right_apply(0, ring.at[0])

    def save(k, carry):
        rfirst[k] = ring[0, k, PAD : PAD + NGY, :]
        return carry

    lax.fori_loop(0, ct, save, 0)

    def step(i, carry):
        now = lax.rem(i + 1, 3)

        @pl.when(i + 1 < rt)
        def _():
            fetch(i + 1).wait()

            @pl.when(i + 3 < rt)
            def _():
                fetch(i + 3).start()

            right_apply(i + 1, ring.at[now])

        @pl.when(i + 1 == rt)
        def _():
            ring[now] = jnp.zeros(ring.shape[1:], F32)

        row_coefs(i)
        mid = lax.rem(i, 3)
        old = lax.rem(i + 2, 3)
        for g in range(groups):
            s = slice(g * RG, (g + 1) * RG)
            c0, c1, c2, c3, c4 = cb[0, s], cb[1, s], cb[2, s], cb[3, s], cb[4, s]
            a0 = PAD + g * RG
            for k in range(ct):
                acc = c0 * ring[mid, k, a0 : a0 + RG] + c1 * ring[old, k, a0 : a0 + RG]
                acc = acc + c2 * ring[now, k, a0 : a0 + RG]
                acc = acc + c3 * ring[mid, k, a0 - 1 : a0 - 1 + RG]
                acc = acc + c4 * ring[mid, k, a0 + 1 : a0 + 1 + RG]
                at = pl.ds(pl.multiple_of(i * NGY + g * RG, RG), RG)
                pred_ref[at, k * NGY : (k + 1) * NGY] = acc
        gx = r * rt + i
        kd = gx - c * ct

        @pl.when((kd >= 0) & (kd < ct))
        def _():
            sub = lax.broadcasted_iota(jnp.int32, (NGY, NGY), 0)
            lan = lax.broadcasted_iota(jnp.int32, (NGY, NGY), 1)
            add = jnp.where(sub == lan, process_ref[pl.ds(gx, 1), :], 0.0)
            rat = pl.ds(pl.multiple_of(i * NGY, NGY), NGY)
            cat = pl.ds(pl.multiple_of(kd * NGY, NGY), NGY)
            pred_ref[rat, cat] = pred_ref[rat, cat] + add

        return carry

    lax.fori_loop(0, rt, step, 0)

    body_rows = pl.ds(PAD, NGY)
    send_up = remote(rfirst, rbot, halo_send.at[0], halo_recv.at[0], r - 1, c)
    send_down = remote(
        ring.at[(rt - 1) % 3, :, body_rows], rtop, halo_send.at[1], halo_recv.at[1], r + 1, c
    )
    pl.when(up)(send_up.start)
    pl.when(down)(send_down.start)

    nchip = ncol // 2
    hop = nchip // 2
    chip, core = c // 2, lax.rem(c, 2)

    def place(q):
        return jnp.where(lax.rem(q, 2) == 0, q // 2, nchip - 1 - q // 2)

    def chip_at(pos):
        pos = lax.rem(pos + nchip, nchip)
        return jnp.where(pos < hop, 2 * pos, 2 * (nchip - 1 - pos) + 1)

    pos, src_pos = place(chip), place(r)
    dist = (lax.rem(pos - src_pos + nchip, nchip), lax.rem(src_pos - pos + nchip, nchip))
    nxt = (chip_at(pos + 1) * 2 + core, chip_at(pos - 1) * 2 + core)
    is_src = dist[0] == 0
    ring_out, swap_out = [], []
    for n in range(nrow):
        z = lax.rem(r + n, nrow)
        if n > 0:
            zat = pl.ds(pl.multiple_of(z * own, own), own)
            remote(across.at[zat], across.at[zat], ac_send.at[0], ac_recv.at[z], z, c).wait_recv()
        for h in range(2):
            at = pl.ds(pl.multiple_of(z * own + h * half, half), half)
            piece = strip_ref.at[core, at]
            fwd = remote(piece, piece, ring_send.at[n, h], ring_recv.at[n, h], r, nxt[h])

            @pl.when(is_src)
            def _():
                strip_ref[core, at, :] = across[at, :]

            @pl.when(jnp.logical_not(is_src))
            def _():
                fwd.wait_recv()

            pl.when(dist[h] < nchip - 1)(fwd.start)
            swap = remote(piece, piece, swap_send.at[n, h], swap_recv.at[n, h], r, c + 1 - 2 * core)
            swap.start()
            ring_out.append((h, fwd))
            swap_out.append(swap)

    low = tmat[:, slots:]
    wt = cols // 2 if cols // 2 % NGY == 0 else cols
    for k in range(cols // wt):
        at = slice(k * wt, (k + 1) * wt)
        y = jnp.dot(low, across[:, at], precision=HIGHEST) * dcol[:, 0:1]
        w_ref[:, at] = coldot(low, y)

    pl.when(down)(send_up.wait_recv)
    pl.when(up)(send_down.wait_recv)
    for side, buf, link, t in ((0, rtop, 0, 0), (1, rbot, 1, rt - 1)):
        gx = r * rt + t
        v = jnp.broadcast_to(links_ref[pl.ds(link * ngx + gx, 1), :], (NGY, NGY)).T
        for k in range(ct):
            rat = slice(t * NGY, (t + 1) * NGY)
            cat = slice(k * NGY, (k + 1) * NGY)
            pred_ref[rat, cat] = pred_ref[rat, cat] + v * buf[k]

    for n in range(nrow):
        z = lax.rem(r + n, nrow)
        for h in range(2):
            at = pl.ds(pl.multiple_of(z * own + h * half, half), half)
            other = strip_ref.at[1 - core, at]
            remote(other, other, swap_send.at[n, h], swap_recv.at[n, h], r, c).wait_recv()
    for h, fwd in ring_out:
        pl.when(dist[h] < nchip - 1)(fwd.wait_send)
    for copy in swap_out + gz_out + ac_out + s_out:
        copy.wait_send()
    for cond_send, cond_recv, copy in small:
        pl.when(cond_send)(copy.wait_send)
    for to_left, to_right in cols_out:
        pl.when(lef)(to_left.wait_send)
        pl.when(rig)(to_right.wait_send)
    pl.when(up)(send_up.wait_send)
    pl.when(down)(send_down.wait_send)


def main(nrow, ncol, cov, bp, sp, ownc, ownp, colc, diag, center, links, process):
    rows, cols = cov.shape
    rt, ct = rows // NGY, cols // NGY
    own = bp.shape[0]
    slots = diag.shape[0]
    nchunk = 4
    vmem = pl.BlockSpec(memory_space=pltpu.VMEM)
    dma = lambda *s: pltpu.SemaphoreType.DMA(s)
    return pl.pallas_call(
        functools.partial(main_kernel, nrow, ncol),
        in_specs=[pl.BlockSpec(memory_space=pl.ANY)] + [vmem] * 9,
        out_specs=[vmem] * 3,
        out_shape=[
            pltpu.VMEM((rows, cols), F32),
            pltpu.VMEM((slots, cols), F32),
            pltpu.VMEM((2, slots, cols), F32),
        ],
        scratch_shapes=[
            pltpu.VMEM((5, ct, NGY), F32),
            pltpu.VMEM((5, NGY, NGY), F32),
            pltpu.VMEM((3, NGY, cols), F32),
            pltpu.VMEM((3, ct, NGY + 2 * PAD, NGY), F32),
            pltpu.VMEM((rows, NGY), F32),
            pltpu.VMEM((rows, NGY), F32),
            pltpu.VMEM((ct, NGY, NGY), F32),
            pltpu.VMEM((ct, NGY, NGY), F32),
            pltpu.VMEM((ct, NGY, NGY), F32),
            pltpu.VMEM((2, WMAX, cols), F32),
            pltpu.VMEM((3, own, NGY), F32),
            pltpu.VMEM((3, own, NGY), F32),
            pltpu.VMEM((slots, cols), F32),
            pltpu.VMEM((nrow, WMAX, NGY), F32),
            pltpu.VMEM((slots, slots), F32),
            pltpu.VMEM((slots, 2 * slots), F32),
            pltpu.VMEM((slots, NGY), F32),
            dma(3), dma(2, nchunk), dma(2, nchunk), dma(2), dma(2), dma(2, 3), dma(2, 3),
            dma(nrow), dma(nrow), dma(ncol), dma(ncol), dma(nrow), dma(nrow), dma(2), dma(2),
            dma(nrow, 2), dma(nrow, 2), dma(nrow, 2), dma(nrow, 2),
        ],
        compiler_params=pltpu.CompilerParams(
            collective_id=0, has_side_effects=True, vmem_limit_bytes=24 * 2**20
        ),
        name="main",
    )(cov, bp, sp, ownc, ownp, colc, diag, center, links, process)


def final_kernel(pred_ref, w_ref, strip_ref, o_ref, whi, wlo):
    i = pl.program_id(0)
    tile = o_ref.shape[0]
    cols = o_ref.shape[1]

    @pl.when(i == 0)
    def _():
        hi = w_ref[...].astype(BF16)
        whi[...] = hi
        wlo[...] = (w_ref[...] - hi.astype(F32)).astype(BF16)

    part = cols // tile
    at = pl.ds(pl.multiple_of(lax.rem(i, part) * tile, tile), tile)
    s = strip_ref[i // part, :, at].T
    hi = s.astype(BF16)
    lo = (s - hi.astype(F32)).astype(BF16)
    dot = functools.partial(jnp.dot, preferred_element_type=F32)
    update = dot(hi, whi[...]) + (dot(lo, whi[...]) + dot(hi, wlo[...]))
    o_ref[...] = pred_ref[pl.ds(pl.multiple_of(i * tile, tile), tile), :] - update


def final(pred, w, strip):
    rows, cols = pred.shape
    tile = 256
    vmem = pl.BlockSpec(memory_space=pltpu.VMEM)
    keep = lambda a: pltpu.with_memory_space_constraint(a, pltpu.VMEM)
    return pl.pallas_call(
        final_kernel,
        grid=(rows // tile,),
        in_specs=[vmem] * 3,
        out_specs=pl.BlockSpec((tile, cols), lambda i: (i, 0)),
        out_shape=jax.ShapeDtypeStruct((rows, cols), F32),
        scratch_shapes=[pltpu.VMEM(w.shape, BF16), pltpu.VMEM(w.shape, BF16)],
        compiler_params=pltpu.CompilerParams(vmem_limit_bytes=20 * 2**20),
        name="final",
    )(keep(pred), keep(w), keep(strip))


def solution(mesh):
    nrow, ncol = mesh.shape["row"], mesh.shape["col"]

    def shards(covariance, center, links, process, wells, noise):
        center = center.reshape(-1, NGY)
        links = links.reshape(-1, NGY)
        process = process.reshape(-1, NGY)
        small = prep(nrow, ncol, wells, noise, center, links, process, covariance)
        return final(*main(nrow, ncol, covariance, *small, center, links, process))

    in_specs = (P("row", "col"), P(), P(), P(), P(), P())
    out_specs = P("row", "col")
    return jax.shard_map(shards, mesh=mesh, in_specs=in_specs, out_specs=out_specs, check_vma=False)
```

```python
import functools

import jax
import jax.numpy as jnp
from jax import lax
from jax.experimental import pallas as pl
from jax.experimental.pallas import tpu as pltpu
from jax.sharding import PartitionSpec as P

NGY = 128
WMAX = 32
PANEL = 32
PAD = 8
RG = 16
SCOPED = 24 * 2**20
HIGHEST = lax.Precision.HIGHEST
F32 = jnp.float32
BF16 = jnp.bfloat16
MESH = pl.DeviceIdType.MESH


def iota(shape, dim):
    return lax.broadcasted_iota(jnp.int32, shape, dim).astype(F32)


def rowdot(a, b, precision=HIGHEST):
    return lax.dot_general(
        a, b, (((1,), (1,)), ((), ())), precision=precision, preferred_element_type=F32
    )


def coldot(a, b, precision=HIGHEST):
    return lax.dot_general(
        a, b, (((0,), (0,)), ((), ())), precision=precision, preferred_element_type=F32
    )


def prep_kernel(
    nrow, wells_ref, noise_ref, center_ref, links_ref, process_ref, cov_ref,
    bp_ref, sp_ref, ownc_ref, ownp_ref, colc_ref, diag_ref,
    tables, cells, rows_v, rows_s, coef, near, spill, idx_sem, near_sem, spill_sem,
):
    rows, cols = cov_ref.shape
    m = wells_ref.shape[1]
    slots = diag_ref.shape[0]
    ngx = center_ref.shape[0]
    own = bp_ref.shape[0]
    span = own + 2 * WMAX
    r = lax.axis_index("row")
    c = lax.axis_index("col")

    w = wells_ref[...].astype(F32)
    block = jnp.floor(w * (1.0 / cols))
    square = jnp.broadcast_to(block, (m, m)).T
    earlier = (square == block) & (iota((m, m), 0) < iota((m, m), 1))
    rank = jnp.sum(jnp.where(earlier, 1.0, 0.0), axis=0, keepdims=True)
    slot = block * WMAX + rank
    onehot = slot == iota((slots, m), 0)
    cell = jnp.sum(jnp.where(onehot, w + 1.0, 0.0), axis=1, keepdims=True) - 1.0
    noise = jnp.sum(jnp.where(onehot, noise_ref[...], 0.0), axis=1, keepdims=True)
    diag_ref[...] = jnp.broadcast_to(jnp.where(cell < 0.0, 1.0, noise), diag_ref.shape)
    cells[...] = jnp.full(cells.shape, -1.0, F32)
    cells[WMAX : WMAX + slots, :] = jnp.broadcast_to(cell, (slots, NGY))

    mine = cells[pl.ds(pl.multiple_of(r * own, WMAX), span), :]
    colc_ref[...] = cells[pl.ds(pl.multiple_of(WMAX + c * WMAX, WMAX), WMAX), :]
    ownc_ref[...] = mine[WMAX : WMAX + own]
    local = mine - (r * rows).astype(F32)
    rows_v[...] = local.T[0:8].astype(jnp.int32)
    copy = pltpu.make_async_copy(rows_v, rows_s, idx_sem)
    copy.start()

    for t in range(6):
        if t == 0:
            tables[:, :NGY] = center_ref[...]
        elif t < 5:
            tables[:, t * NGY : (t + 1) * NGY] = links_ref[(t - 1) * ngx : t * ngx, :]
        else:
            tables[:, t * NGY : (t + 1) * NGY] = process_ref[...]
    gx = jnp.floor(mine[:, :1] * (1.0 / NGY))
    gy = mine[:, :1] - gx * NGY
    pickx = jnp.where(gx == iota((span, ngx), 1), 1.0, 0.0)
    table = jnp.dot(pickx, tables[...], precision=HIGHEST)
    copy.wait()

    moves = (0, -NGY, NGY, -1, 1)

    def row(i):
        return cov_ref.at[pl.ds(jnp.clip(i, 0, rows - 1), 1), :]

    def gather(i, carry):
        at = rows_s[0, WMAX + i]
        for t in range(5):
            dst = near.at[pl.ds(t * own + i, 1), :]
            pltpu.make_async_copy(row(at + moves[t]), dst, near_sem).start()
        return carry

    lax.fori_loop(0, own, gather, 0)

    def gather_spill(i, carry):
        low = spill.at[pl.ds(i, 1), :]
        high = spill.at[pl.ds(WMAX + i, 1), :]
        pltpu.make_async_copy(row(rows_s[0, i] + NGY), low, spill_sem).start()
        pltpu.make_async_copy(row(rows_s[0, WMAX + own + i] - NGY), high, spill_sem).start()
        return carry

    lax.fori_loop(0, WMAX, gather_spill, 0)

    picky = gy == iota((span, NGY), 1)
    valid = mine[:, :1] >= 0.0
    lv = local[:, :1]
    for t in range(5):
        value = jnp.sum(
            jnp.where(picky, table[:, t * NGY : (t + 1) * NGY], 0.0), axis=1, keepdims=True
        )
        target = lv + moves[t]
        ok = valid & (target >= 0.0) & (target < rows)
        if t == 3:
            ok = ok & (gy > 0.0)
        if t == 4:
            ok = ok & (gy < NGY - 1.0)
        coef[t] = jnp.broadcast_to(jnp.where(ok, value, 0.0), (span, NGY))
    value = jnp.sum(jnp.where(picky, table[:, 5 * NGY :], 0.0), axis=1, keepdims=True)
    value = jnp.where(valid, value, 0.0)
    ownp_ref[...] = jnp.broadcast_to(value[WMAX : WMAX + own], (own, NGY))

    pltpu.make_async_copy(cov_ref.at[pl.ds(0, 5 * own), :], near, near_sem).wait()
    pltpu.make_async_copy(cov_ref.at[pl.ds(0, 2 * WMAX), :], spill, spill_sem).wait()
    for k in range(cols // NGY):
        at = slice(k * NGY, (k + 1) * NGY)
        acc = coef[0, WMAX : WMAX + own] * near[0:own, at]
        for t in range(1, 5):
            acc = acc + coef[t, WMAX : WMAX + own] * near[t * own : (t + 1) * own, at]
        bp_ref[:, at] = acc
        sp_ref[:WMAX, at] = coef[2, :WMAX] * spill[:WMAX, at]
        sp_ref[WMAX:, at] = coef[1, WMAX + own :] * spill[WMAX:, at]


def keep(a):
    return pltpu.with_memory_space_constraint(a, pltpu.VMEM)


def prep(nrow, ncol, wells, noise, center, links, process, cov):
    rows, cols = cov.shape
    ratio = rows // cols
    own = ratio * WMAX
    slots = ncol * WMAX
    span = own + 2 * WMAX
    m = wells.shape[1]
    vmem = pl.BlockSpec(memory_space=pltpu.VMEM)
    out = lambda *s: pltpu.HBM(s, F32)
    return pl.pallas_call(
        functools.partial(prep_kernel, nrow),
        in_specs=[vmem] * 5 + [pl.BlockSpec(memory_space=pltpu.HBM)],
        out_specs=[vmem] * 6,
        out_shape=[
            out(own, cols), out(2 * WMAX, cols), out(own, NGY), out(own, NGY),
            out(WMAX, NGY), out(slots, NGY),
        ],
        scratch_shapes=[
            pltpu.VMEM((center.shape[0], 6 * NGY), F32),
            pltpu.VMEM((slots + 2 * WMAX, NGY), F32),
            pltpu.VMEM((8, span), jnp.int32),
            pltpu.SMEM((8, span), jnp.int32),
            pltpu.VMEM((5, span, NGY), F32),
            pltpu.VMEM((5 * own, cols), F32),
            pltpu.VMEM((2 * WMAX, cols), F32),
            pltpu.SemaphoreType.DMA,
            pltpu.SemaphoreType.DMA,
            pltpu.SemaphoreType.DMA,
        ],
        compiler_params=pltpu.CompilerParams(vmem_limit_bytes=SCOPED),
        name="prep",
    )(wells, noise, center, links, process, cov)


def main_kernel(
    nrow, ncol, pieces, pace,
    cov_ref, bp_ref, sp_ref, ownc_ref, ownp_ref, colc_ref, diag_ref,
    center_ref, links_ref, process_ref,
    pred_ref, across, strip_ref,
    ccol, rowt, xbuf, even, odd, lh, rh, rtop, rbot, rfirst, rlast,
    spin, hl, hr, gz, smat, tmat, dcol,
    x_sem, col_send, col_recv, spin_send, spin_recv, edge_send, edge_recv,
    gz_send, gz_recv, s_send, s_recv, ac_send, ac_recv, halo_send, halo_recv,
    ring_send, ring_recv, swap_send, swap_recv,
):
    rows, cols = cov_ref.shape
    rt = rows // NGY
    ct = cols // NGY
    own = bp_ref.shape[0]
    slots = across.shape[0]
    ngx = center_ref.shape[0]
    r = lax.axis_index("row")
    c = lax.axis_index("col")
    up, down = r > 0, r < nrow - 1
    lef, rig = c > 0, c < ncol - 1
    one = lambda cond: jnp.where(cond, 1, 0)

    def remote(src, dst, ssem, rsem, dr, dc):
        return pltpu.make_async_remote_copy(
            src_ref=src, dst_ref=dst, send_sem=ssem, recv_sem=rsem,
            device_id={"row": dr, "col": dc}, device_id_type=MESH,
        )

    base = pl.multiple_of(c * ct, 8)
    lane = lax.broadcasted_iota(jnp.int32, (ct, NGY), 1)
    ccol[0] = center_ref[pl.ds(base, ct), :]
    for t in range(4):
        v = links_ref[pl.ds(pl.multiple_of(t * ngx + base, 8), ct), :]
        if t == 2:
            v = jnp.where(lane == 0, 0.0, v)
        if t == 3:
            v = jnp.where(lane == NGY - 1, 0.0, v)
        ccol[t + 1] = v

    sub = lax.broadcasted_iota(jnp.int32, (NGY, ngx), 0)
    for t in range(5):
        v = (center_ref[...] if t == 0 else links_ref[(t - 1) * ngx : t * ngx, :]).T
        if t == 3:
            v = jnp.where(sub == 0, 0.0, v)
        if t == 4:
            v = jnp.where(sub == NGY - 1, 0.0, v)
        rowt[t] = v

    even[...] = jnp.zeros(even.shape, F32)
    odd[...] = jnp.zeros(odd.shape, F32)

    @pl.when(r == 0)
    def _():
        rtop[...] = jnp.zeros(rtop.shape, F32)
        spin[0] = jnp.zeros(spin.shape[1:], F32)
        hl[1] = jnp.zeros(hl.shape[1:], F32)
        hr[1] = jnp.zeros(hr.shape[1:], F32)

    @pl.when(r == nrow - 1)
    def _():
        rbot[...] = jnp.zeros(rbot.shape, F32)
        spin[1] = jnp.zeros(spin.shape[1:], F32)
        hl[2] = jnp.zeros(hl.shape[1:], F32)
        hr[2] = jnp.zeros(hr.shape[1:], F32)

    @pl.when(c == 0)
    def _():
        lh[...] = jnp.zeros(lh.shape, F32)
        hl[...] = jnp.zeros(hl.shape, F32)

    @pl.when(c == ncol - 1)
    def _():
        rh[...] = jnp.zeros(rh.shape, F32)
        hr[...] = jnp.zeros(hr.shape, F32)

    bar = pltpu.get_barrier_semaphore()

    def greet(dr, dc):
        pl.semaphore_signal(bar, 1, device_id={"row": dr, "col": dc}, device_id_type=MESH)

    for d in range(1, nrow):
        greet(lax.rem(r + d, nrow), c)
    for d in range(1, ncol):
        greet(r, lax.rem(c + d, ncol))
    for dr, okr in ((-1, up), (1, down)):
        for dc, okc in ((-1, lef), (1, rig)):
            @pl.when(okr & okc)
            def _():
                greet(r + dr, c + dc)
    diagonals = (one(up) + one(down)) * (one(lef) + one(rig))
    pl.semaphore_wait(bar, nrow - 1 + ncol - 1 + diagonals)

    half_rows = lambda k: pl.ds(k * WMAX, WMAX)
    small = []

    def exchange(cond_send, cond_recv, src, dst, ssem, rsem, dr, dc):
        copy = remote(src, dst, ssem, rsem, dr, dc)
        pl.when(cond_send)(copy.start)
        small.append((cond_send, cond_recv, copy))

    exchange(up, down, sp_ref.at[half_rows(0)], spin.at[1], spin_send.at[0], spin_recv.at[0], r - 1, c)
    exchange(down, up, sp_ref.at[half_rows(1)], spin.at[0], spin_send.at[1], spin_recv.at[1], r + 1, c)
    for side, ok, no, buf, dc in ((0, lef, rig, hr, -1), (1, rig, lef, hl, 1)):
        at = slice(0, NGY) if side == 0 else slice(cols - NGY, cols)
        exchange(ok, no, bp_ref.at[:, at], buf.at[0], edge_send.at[side, 0], edge_recv.at[side, 0], r, c + dc)
        exchange(
            up & ok, down & no, sp_ref.at[half_rows(0), at], buf.at[2, half_rows(0)],
            edge_send.at[side, 1], edge_recv.at[side, 1], r - 1, c + dc,
        )
        exchange(
            down & ok, up & no, sp_ref.at[half_rows(1), at], buf.at[1, half_rows(0)],
            edge_send.at[side, 2], edge_recv.at[side, 2], r + 1, c + dc,
        )

    def fetch(t):
        b = lax.rem(t, 3)
        return pltpu.make_async_copy(
            cov_ref.at[pl.ds(pl.multiple_of(t * NGY, NGY), NGY), :], xbuf.at[b], x_sem.at[b]
        )

    fetch(0).start()
    fetch(1).start()

    for cond_send, cond_recv, copy in small:
        pl.when(cond_recv)(copy.wait_recv)

    mine = pl.ds(pl.multiple_of(r * own, own), own)

    def total(k):
        if k < 0:
            main, top, bottom = hl[0], hl[1, 0:WMAX], hl[2, 0:WMAX]
        elif k == ct:
            main, top, bottom = hr[0], hr[1, 0:WMAX], hr[2, 0:WMAX]
        else:
            at = slice(k * NGY, (k + 1) * NGY)
            main, top, bottom = bp_ref[:, at], spin[0, :, at], spin[1, :, at]
        if own == 2 * WMAX:
            return main + jnp.concatenate([top, bottom], axis=0)
        gap = jnp.zeros((own - 2 * WMAX, NGY), F32)
        return main + jnp.concatenate([top, gap, bottom], axis=0)

    cell_at = ownc_ref[...] - (c * cols).astype(F32)
    before, here = total(-1), total(0)
    for k in range(ct):
        after = total(k + 1)
        acc = ccol[0, k : k + 1] * here + ccol[1, k : k + 1] * before + ccol[2, k : k + 1] * after
        acc = acc + ccol[3, k : k + 1] * pltpu.roll(here, 1, 1)
        acc = acc + ccol[4, k : k + 1] * pltpu.roll(here, NGY - 1, 1)
        hit = cell_at == iota((own, NGY), 1) + k * NGY
        acc = acc + jnp.where(hit, ownp_ref[...], 0.0)
        across[mine, k * NGY : (k + 1) * NGY] = acc
        before, here = here, after

    pick_at = colc_ref[...] - (c * cols).astype(F32)
    gram = jnp.zeros((WMAX, own), F32)
    for k in range(ct):
        pick = jnp.where(pick_at == iota((WMAX, NGY), 1) + k * NGY, 1.0, 0.0)
        gram = gram + rowdot(pick, across[mine, k * NGY : (k + 1) * NGY])
    gz[r, :, 0:own] = gram

    gz_out, ac_out = [], []
    for d in range(1, nrow):
        peer = lax.rem(r + d, nrow)
        copy = remote(gz.at[r], gz.at[r], gz_send.at[d - 1], gz_recv.at[r], peer, c)
        copy.start()
        gz_out.append(copy)
    for d in range(1, nrow):
        peer = lax.rem(r + d, nrow)
        copy = remote(across.at[mine], across.at[mine], ac_send.at[d - 1], ac_recv.at[r], peer, c)
        copy.start()
        ac_out.append(copy)
    for d in range(1, nrow):
        src = lax.rem(r + d, nrow)
        remote(gz.at[src], gz.at[src], gz_send.at[0], gz_recv.at[src], src, c).wait_recv()
    srow = pl.ds(pl.multiple_of(c * WMAX, WMAX), WMAX)
    for j in range(nrow):
        smat[srow, j * own : (j + 1) * own] = gz[j, :, 0:own]
    s_out = []
    for d in range(1, ncol):
        peer = lax.rem(c + d, ncol)
        copy = remote(smat.at[srow], smat.at[srow], s_send.at[d - 1], s_recv.at[c], r, peer)
        copy.start()
        s_out.append(copy)
    for d in range(1, ncol):
        src = lax.rem(c + d, ncol)
        at = pl.ds(pl.multiple_of(src * WMAX, WMAX), WMAX)
        remote(smat.at[at], smat.at[at], s_send.at[0], s_recv.at[src], r, src).wait_recv()

    cols_out = []
    for n, (t0, tiles) in enumerate(pieces):
        at = pl.ds(t0 * NGY, tiles * NGY)
        to_left = remote(cov_ref.at[at, 0:NGY], rh.at[at], col_send.at[0, n], col_recv.at[0, n], r, c - 1)
        to_right = remote(
            cov_ref.at[at, cols - NGY : cols], lh.at[at], col_send.at[1, n], col_recv.at[1, n], r, c + 1
        )
        pl.when(lef)(to_left.start)
        pl.when(rig)(to_right.start)
        cols_out.append((to_left, to_right))

    eye = iota((slots, slots), 0) == iota((slots, slots), 1)
    for k in range(slots // NGY):
        at = slice(k * NGY, (k + 1) * NGY)
        tmat[:, at] = smat[:, at] + jnp.where(eye[:, at], diag_ref[...], 0.0)
    tmat[:, slots:] = jnp.where(eye, 1.0, 0.0)
    lanes = lax.broadcasted_iota(jnp.int32, (PANEL, NGY), 1)
    subs = lax.broadcasted_iota(jnp.int32, (PANEL, NGY), 0)

    def panel(p, carry):
        at = pl.ds(pl.multiple_of(p * PANEL, PANEL), PANEL)
        per = NGY // PANEL
        block = tmat[at, 0:NGY]
        for t in range(1, slots // NGY):
            block = jnp.where(p // per == t, tmat[at, t * NGY : (t + 1) * NGY], block)
        block = pltpu.roll(block, lax.rem(per - lax.rem(p, per), per) * PANEL, 1)
        a = jnp.where(lanes < PANEL, block, jnp.where(lanes - PANEL == subs, 1.0, 0.0))
        for k in range(PANEL - 1):
            row = a[k : k + 1, :]
            col = jnp.where(subs > k, jnp.broadcast_to(a[:, k : k + 1], (PANEL, NGY)), 0.0)
            pivot = jnp.broadcast_to(row[:, k : k + 1], (1, NGY))
            a = a - col * (row / pivot)
        pivots = jnp.sum(jnp.where(lanes == subs, a, 0.0), axis=1, keepdims=True)
        dinv = jnp.broadcast_to(1.0 / pivots, (PANEL, NGY))
        dcol[at, :] = dinv
        low = pltpu.roll(a, NGY - PANEL, 1)[:, 0:PANEL]
        u = jnp.dot(low, tmat[at, :], precision=HIGHEST)
        tmat[at, :] = u
        right = lax.broadcasted_iota(jnp.int32, (PANEL, slots), 1) >= (p + 1) * PANEL
        x = jnp.where(right, u[:, 0:slots] * dinv[:, 0:1], 0.0)
        tmat[...] = tmat[...] - coldot(x, u)
        return carry

    lax.fori_loop(0, slots // PANEL, panel, 0)

    nchip = ncol // 2
    hop = nchip // 2
    chip, core = c // 2, lax.rem(c, 2)

    def place(q):
        return jnp.where(lax.rem(q, 2) == 0, q // 2, nchip - 1 - q // 2)

    def chip_at(pos):
        pos = lax.rem(pos + nchip, nchip)
        return jnp.where(pos < hop, 2 * pos, 2 * (nchip - 1 - pos) + 1)

    pos, src_pos = place(chip), place(r)
    dist = (lax.rem(pos - src_pos + nchip, nchip), lax.rem(src_pos - pos + nchip, nchip))
    nxt = (chip_at(pos + 1) * 2 + core, chip_at(pos - 1) * 2 + core)
    is_src = dist[0] == 0
    count = 2 * nrow
    turns = count + nchip - 1
    share = (own // 4 // 2, own * 3 // 4 // 2)

    def wait_across(z):
        zat = pl.ds(pl.multiple_of(z * own, own), own)
        remote(across.at[zat], across.at[zat], ac_send.at[0], ac_recv.at[z], z, c).wait_recv()

    def moves(n, h):
        z = lax.rem(r + n // 2, nrow)
        start = z * own + h * 2 * share[0] + lax.rem(n, 2) * share[h]
        at = pl.ds(pl.multiple_of(start, 8), share[h])
        here, there = strip_ref.at[core, at], strip_ref.at[1 - core, at]
        fwd = remote(here, here, ring_send.at[h, n], ring_recv.at[h, n], r, nxt[h])
        swap = remote(here, here, swap_send.at[h, n], swap_recv.at[h, n], r, c + 1 - 2 * core)
        back = remote(there, there, swap_send.at[h, n], swap_recv.at[h, n], r, c + 1 - 2 * core)
        return at, fwd, swap, back

    def relay(t):
        @pl.when(is_src & (lax.rem(t, 2) == 0) & (t >= 2) & (t < count))
        def _():
            wait_across(lax.rem(r + t // 2, nrow))

        for h in range(2):
            n = t - dist[h]

            @pl.when((n >= 0) & (n < count))
            def _():
                at, fwd, swap, _ = moves(n, h)

                @pl.when(is_src)
                def _():
                    strip_ref[core, at, :] = across[at, :]

                @pl.when(jnp.logical_not(is_src))
                def _():
                    fwd.wait_recv()

                pl.when(dist[h] < nchip - 1)(fwd.start)
                swap.start()

    groups = NGY // RG

    def right_group(t, b, g, k, before, here):
        at = pl.ds(pl.multiple_of(g * RG, RG), RG)
        gat = pl.ds(pl.multiple_of(t * NGY + g * RG, RG), RG)
        if k < 0:
            return lh[gat, :], xbuf[b, at, 0:NGY]
        after = xbuf[b, at, (k + 1) * NGY : (k + 2) * NGY] if k < ct - 1 else rh[gat, :]
        acc = ccol[0, k : k + 1] * here + ccol[1, k : k + 1] * before + ccol[2, k : k + 1] * after
        acc = acc + ccol[3, k : k + 1] * pltpu.roll(here, 1, 1)
        acc = acc + ccol[4, k : k + 1] * pltpu.roll(here, NGY - 1, 1)
        return here, after, acc

    def right_apply(t, b, dst, pad):
        def body(g, carry):
            before, here = right_group(t, b, g, -1, None, None)
            for k in range(ct):
                before, here, acc = right_group(t, b, g, k, before, here)
                dst[k, pl.ds(pl.multiple_of(pad + g * RG, 8), RG), :] = acc
            return carry

        lax.fori_loop(0, groups, body, 0)

    def left_apply(i, mid, other, following):
        gx = r * rt + i
        turn = lax.rem(ngx - gx, ngx)
        b = lax.rem(i + 1, 3)

        def body(g, carry):
            s = pl.ds(pl.multiple_of(g * RG, RG), RG)
            c0, c1, c2, c3, c4 = [
                jnp.broadcast_to(pltpu.roll(rowt[t, s], turn, 1)[:, 0:1], (RG, NGY)) for t in range(5)
            ]
            a0 = PAD + g * RG
            same = pl.ds(pl.multiple_of(a0, 8), RG)
            above = pl.ds(a0 - 1, RG)
            below = pl.ds(a0 + 1, RG)
            at = pl.ds(pl.multiple_of(i * NGY + g * RG, RG), RG)
            if following:
                before, here = right_group(i + 1, b, g, -1, None, None)
            for k in range(ct):
                acc = c0 * mid[k, same] + c1 * other[k, same]
                acc = acc + c3 * mid[k, above] + c4 * mid[k, below]
                if following:
                    before, here, nxt_row = right_group(i + 1, b, g, k, before, here)
                    other[k, same] = nxt_row
                    acc = acc + c2 * nxt_row
                pred_ref[at, k * NGY : (k + 1) * NGY] = acc
            return carry

        lax.fori_loop(0, groups, body, 0)

    def add_process(i):
        gx = r * rt + i
        kd = gx - c * ct

        @pl.when((kd >= 0) & (kd < ct))
        def _():
            sub = lax.broadcasted_iota(jnp.int32, (NGY, NGY), 0)
            lan = lax.broadcasted_iota(jnp.int32, (NGY, NGY), 1)
            add = jnp.where(sub == lan, process_ref[pl.ds(gx, 1), :], 0.0)
            rat = pl.ds(pl.multiple_of(i * NGY, NGY), NGY)
            cat = pl.ds(pl.multiple_of(kd * NGY, NGY), NGY)
            pred_ref[rat, cat] = pred_ref[rat, cat] + add

    def wait_cols(n):
        pl.when(rig)(cols_out[n][0].wait_recv)
        pl.when(lef)(cols_out[n][1].wait_recv)

    wait_cols(0)
    wait_cols(1)
    last = pltpu.make_async_copy(cov_ref.at[pl.ds(rows - NGY, NGY), :], xbuf.at[2], x_sem.at[2])
    last.start()
    fetch(0).wait()
    right_apply(0, 0, even, PAD)
    last.wait()
    right_apply(rt - 1, 2, rlast, 0)
    fetch(2).start()

    def save(k, carry):
        rfirst[k] = even[k, PAD : PAD + NGY, :]
        return carry

    lax.fori_loop(0, ct, save, 0)

    send_up = remote(rfirst, rbot, halo_send.at[0], halo_recv.at[0], r - 1, c)
    send_down = remote(
        rlast, rtop, halo_send.at[1], halo_recv.at[1], r + 1, c
    )

    def step(i, mid, other):
        for n in range(2, len(pieces)):
            pl.when(i + 1 == pieces[n][0])(functools.partial(wait_cols, n))

        @pl.when(i == rt // 4)
        def _():
            pl.when(up)(send_up.start)
            pl.when(down)(send_down.start)

        pl.when(lax.rem(i, pace) == 0)(functools.partial(relay, i // pace))
        fetch(i + 1).wait()

        @pl.when(i + 3 < rt)
        def _():
            fetch(i + 3).start()

        left_apply(i, mid, other, True)
        add_process(i)

    def pair(p, carry):
        step(2 * p, even, odd)
        step(2 * p + 1, odd, even)
        return carry

    lax.fori_loop(0, (rt - 2) // 2, pair, 0)
    step(rt - 2, even, odd)
    left_apply(rt - 1, odd, even, False)
    add_process(rt - 1)

    def finish(t, carry):
        relay(t)
        return carry

    lax.fori_loop(-(-rt // pace), turns, finish, 0)
    for d in range(1, nrow):
        z = lax.rem(r + d, nrow)

        @pl.when(jnp.logical_not(is_src))
        def _():
            wait_across(z)

    for copy in ac_out:
        copy.wait_send()
    low = tmat[:, slots:]
    wt = cols // 2 if cols // 2 % NGY == 0 else cols
    for k in range(cols // wt):
        at = slice(k * wt, (k + 1) * wt)
        y = jnp.dot(low, across[:, at], precision=HIGHEST) * dcol[:, 0:1]
        across[:, at] = coldot(low, y)

    pl.when(down)(send_up.wait_recv)
    pl.when(up)(send_down.wait_recv)
    for side, buf, link, t in ((0, rtop, 0, 0), (1, rbot, 1, rt - 1)):
        gx = r * rt + t
        v = jnp.broadcast_to(links_ref[pl.ds(link * ngx + gx, 1), :], (NGY, NGY)).T
        for k in range(ct):
            rat = slice(t * NGY, (t + 1) * NGY)
            cat = slice(k * NGY, (k + 1) * NGY)
            pred_ref[rat, cat] = pred_ref[rat, cat] + v * buf[k]

    def drain(n, carry):
        for h in range(2):
            _, fwd, swap, back = moves(n, h)
            back.wait_recv()
            swap.wait_send()
            pl.when(dist[h] < nchip - 1)(fwd.wait_send)
        return carry

    lax.fori_loop(0, count, drain, 0)
    for copy in gz_out + s_out:
        copy.wait_send()
    for cond_send, cond_recv, copy in small:
        pl.when(cond_send)(copy.wait_send)
    for to_left, to_right in cols_out:
        pl.when(lef)(to_left.wait_send)
        pl.when(rig)(to_right.wait_send)
    pl.when(up)(send_up.wait_send)
    pl.when(down)(send_down.wait_send)


def main(nrow, ncol, cov, bp, sp, ownc, ownp, colc, diag, center, links, process):
    rows, cols = cov.shape
    rt, ct = rows // NGY, cols // NGY
    own = bp.shape[0]
    slots = diag.shape[0]
    middle = list(range(1, rt - 1, 5)) + [rt - 1]
    pieces = [(0, 1), (rt - 1, 1)] + [(a, b - a) for a, b in zip(middle, middle[1:])]
    nchunk = len(pieces)
    pace = 3
    vmem = pl.BlockSpec(memory_space=pltpu.VMEM)
    dma = lambda *s: pltpu.SemaphoreType.DMA(s)
    return pl.pallas_call(
        functools.partial(main_kernel, nrow, ncol, tuple(pieces), pace),
        in_specs=[pl.BlockSpec(memory_space=pltpu.HBM)] + [vmem] * 9,
        out_specs=[vmem] * 3,
        out_shape=[
            pltpu.VMEM((rows, cols), F32),
            pltpu.VMEM((slots, cols), F32),
            pltpu.VMEM((2, slots, cols), F32),
        ],
        scratch_shapes=[
            pltpu.VMEM((5, ct, NGY), F32),
            pltpu.VMEM((5, NGY, center.shape[0]), F32),
            pltpu.VMEM((3, NGY, cols), F32),
            pltpu.VMEM((ct, NGY + 2 * PAD, NGY), F32),
            pltpu.VMEM((ct, NGY + 2 * PAD, NGY), F32),
            pltpu.VMEM((rows, NGY), F32),
            pltpu.VMEM((rows, NGY), F32),
            pltpu.VMEM((ct, NGY, NGY), F32),
            pltpu.VMEM((ct, NGY, NGY), F32),
            pltpu.VMEM((ct, NGY, NGY), F32),
            pltpu.VMEM((ct, NGY, NGY), F32),
            pltpu.VMEM((2, WMAX, cols), F32),
            pltpu.VMEM((3, own, NGY), F32),
            pltpu.VMEM((3, own, NGY), F32),
            pltpu.VMEM((nrow, WMAX, NGY), F32),
            pltpu.VMEM((slots, slots), F32),
            pltpu.VMEM((slots, 2 * slots), F32),
            pltpu.VMEM((slots, NGY), F32),
            dma(3), dma(2, nchunk), dma(2, nchunk), dma(2), dma(2), dma(2, 3), dma(2, 3),
            dma(nrow), dma(nrow), dma(ncol), dma(ncol), dma(nrow), dma(nrow), dma(2), dma(2),
            dma(2, 2 * nrow), dma(2, 2 * nrow), dma(2, 2 * nrow), dma(2, 2 * nrow),
        ],
        compiler_params=pltpu.CompilerParams(
            collective_id=0, has_side_effects=True, vmem_limit_bytes=SCOPED
        ),
        name="main",
    )(cov, bp, sp, ownc, ownp, colc, diag, center, links, process)


def final_kernel(pred_ref, w_ref, strip_ref, o_ref, whi, wlo):
    i = pl.program_id(0)
    tile = o_ref.shape[0]
    cols = o_ref.shape[1]

    @pl.when(i == 0)
    def _():
        hi = w_ref[...].astype(BF16)
        whi[...] = hi
        wlo[...] = (w_ref[...] - hi.astype(F32)).astype(BF16)

    part = cols // tile
    at = pl.ds(pl.multiple_of(lax.rem(i, part) * tile, tile), tile)
    s = strip_ref[i // part, :, at].T
    hi = s.astype(BF16)
    lo = (s - hi.astype(F32)).astype(BF16)
    dot = functools.partial(jnp.dot, preferred_element_type=F32)
    update = dot(hi, whi[...]) + (dot(lo, whi[...]) + dot(hi, wlo[...]))
    o_ref[...] = pred_ref[pl.ds(pl.multiple_of(i * tile, tile), tile), :] - update


def final(pred, w, strip):
    rows, cols = pred.shape
    tile = 256
    vmem = pl.BlockSpec(memory_space=pltpu.VMEM)
    return pl.pallas_call(
        final_kernel,
        grid=(rows // tile,),
        in_specs=[vmem] * 3,
        out_specs=pl.BlockSpec((tile, cols), lambda i: (i, 0)),
        out_shape=jax.ShapeDtypeStruct((rows, cols), F32),
        scratch_shapes=[pltpu.VMEM(w.shape, BF16), pltpu.VMEM(w.shape, BF16)],
        compiler_params=pltpu.CompilerParams(vmem_limit_bytes=SCOPED),
        name="final",
    )(keep(pred), keep(w), keep(strip))


def solution(mesh):
    nrow, ncol = mesh.shape["row"], mesh.shape["col"]

    def shards(covariance, center, links, process, wells, noise):
        center = center.reshape(-1, NGY)
        links = links.reshape(-1, NGY)
        process = process.reshape(-1, NGY)
        small = prep(nrow, ncol, wells, noise, center, links, process, covariance)
        return final(*main(nrow, ncol, covariance, *small, center, links, process))

    in_specs = (P("row", "col"), P(), P(), P(), P(), P())
    out_specs = P("row", "col")
    return jax.shard_map(shards, mesh=mesh, in_specs=in_specs, out_specs=out_specs, check_vma=False)
```

```python
import functools

import jax
import jax.numpy as jnp
from jax import lax
from jax.experimental import pallas as pl
from jax.experimental.pallas import tpu as pltpu
from jax.sharding import PartitionSpec as P

NGY = 128
WMAX = 32
PANEL = 16
PAD = 8
RG = 16
SCOPED = 24 * 2**20
HIGHEST = lax.Precision.HIGHEST
F32 = jnp.float32
BF16 = jnp.bfloat16
MESH = pl.DeviceIdType.MESH


def iota(shape, dim):
    return lax.broadcasted_iota(jnp.int32, shape, dim).astype(F32)


def rowdot(a, b, precision=HIGHEST):
    return lax.dot_general(
        a, b, (((1,), (1,)), ((), ())), precision=precision, preferred_element_type=F32
    )


def coldot(a, b, precision=HIGHEST):
    return lax.dot_general(
        a, b, (((0,), (0,)), ((), ())), precision=precision, preferred_element_type=F32
    )


def prep_kernel(
    nrow, wells_ref, noise_ref, center_ref, links_ref, process_ref, cov_ref,
    bp_ref, sp_ref, ownc_ref, ownp_ref, colc_ref, diag_ref,
    tables, cells, rows_v, rows_s, coef, near, spill, idx_sem, near_sem, spill_sem,
):
    rows, cols = cov_ref.shape
    m = wells_ref.shape[1]
    slots = diag_ref.shape[0]
    ngx = center_ref.shape[0]
    own = bp_ref.shape[0]
    span = own + 2 * WMAX
    r = lax.axis_index("row")
    c = lax.axis_index("col")

    w = wells_ref[...].astype(F32)
    block = jnp.floor(w * (1.0 / cols))
    square = jnp.broadcast_to(block, (m, m)).T
    earlier = (square == block) & (iota((m, m), 0) < iota((m, m), 1))
    rank = jnp.sum(jnp.where(earlier, 1.0, 0.0), axis=0, keepdims=True)
    slot = block * WMAX + rank
    onehot = slot == iota((slots, m), 0)
    cell = jnp.sum(jnp.where(onehot, w + 1.0, 0.0), axis=1, keepdims=True) - 1.0
    noise = jnp.sum(jnp.where(onehot, noise_ref[...], 0.0), axis=1, keepdims=True)
    diag_ref[...] = jnp.broadcast_to(jnp.where(cell < 0.0, 1.0, noise), diag_ref.shape)
    cells[...] = jnp.full(cells.shape, -1.0, F32)
    cells[WMAX : WMAX + slots, :] = jnp.broadcast_to(cell, (slots, NGY))

    mine = cells[pl.ds(pl.multiple_of(r * own, WMAX), span), :]
    colc_ref[...] = cells[pl.ds(pl.multiple_of(WMAX + c * WMAX, WMAX), WMAX), :]
    ownc_ref[...] = mine[WMAX : WMAX + own]
    local = mine - (r * rows).astype(F32)
    rows_v[...] = local.T[0:8].astype(jnp.int32)
    copy = pltpu.make_async_copy(rows_v, rows_s, idx_sem)
    copy.start()

    for t in range(6):
        if t == 0:
            tables[:, :NGY] = center_ref[...]
        elif t < 5:
            tables[:, t * NGY : (t + 1) * NGY] = links_ref[(t - 1) * ngx : t * ngx, :]
        else:
            tables[:, t * NGY : (t + 1) * NGY] = process_ref[...]
    gx = jnp.floor(mine[:, :1] * (1.0 / NGY))
    gy = mine[:, :1] - gx * NGY
    pickx = jnp.where(gx == iota((span, ngx), 1), 1.0, 0.0)
    table = jnp.dot(pickx, tables[...], precision=HIGHEST)
    copy.wait()

    moves = (0, -NGY, NGY, -1, 1)

    def row(i):
        return cov_ref.at[pl.ds(jnp.clip(i, 0, rows - 1), 1), :]

    def gather(i, carry):
        at = rows_s[0, WMAX + i]
        for t in range(5):
            dst = near.at[pl.ds(t * own + i, 1), :]
            pltpu.make_async_copy(row(at + moves[t]), dst, near_sem).start()
        return carry

    lax.fori_loop(0, own, gather, 0)

    def gather_spill(i, carry):
        low = spill.at[pl.ds(i, 1), :]
        high = spill.at[pl.ds(WMAX + i, 1), :]
        pltpu.make_async_copy(row(rows_s[0, i] + NGY), low, spill_sem).start()
        pltpu.make_async_copy(row(rows_s[0, WMAX + own + i] - NGY), high, spill_sem).start()
        return carry

    lax.fori_loop(0, WMAX, gather_spill, 0)

    picky = gy == iota((span, NGY), 1)
    valid = mine[:, :1] >= 0.0
    lv = local[:, :1]
    for t in range(5):
        value = jnp.sum(
            jnp.where(picky, table[:, t * NGY : (t + 1) * NGY], 0.0), axis=1, keepdims=True
        )
        target = lv + moves[t]
        ok = valid & (target >= 0.0) & (target < rows)
        if t == 3:
            ok = ok & (gy > 0.0)
        if t == 4:
            ok = ok & (gy < NGY - 1.0)
        coef[t] = jnp.broadcast_to(jnp.where(ok, value, 0.0), (span, NGY))
    value = jnp.sum(jnp.where(picky, table[:, 5 * NGY :], 0.0), axis=1, keepdims=True)
    value = jnp.where(valid, value, 0.0)
    ownp_ref[...] = jnp.broadcast_to(value[WMAX : WMAX + own], (own, NGY))

    pltpu.make_async_copy(cov_ref.at[pl.ds(0, 5 * own), :], near, near_sem).wait()
    pltpu.make_async_copy(cov_ref.at[pl.ds(0, 2 * WMAX), :], spill, spill_sem).wait()
    for k in range(cols // NGY):
        at = slice(k * NGY, (k + 1) * NGY)
        acc = coef[0, WMAX : WMAX + own] * near[0:own, at]
        for t in range(1, 5):
            acc = acc + coef[t, WMAX : WMAX + own] * near[t * own : (t + 1) * own, at]
        bp_ref[:, at] = acc
        sp_ref[:WMAX, at] = coef[2, :WMAX] * spill[:WMAX, at]
        sp_ref[WMAX:, at] = coef[1, WMAX + own :] * spill[WMAX:, at]


def keep(a):
    return pltpu.with_memory_space_constraint(a, pltpu.VMEM)


def prep(nrow, ncol, wells, noise, center, links, process, cov):
    rows, cols = cov.shape
    ratio = rows // cols
    own = ratio * WMAX
    slots = ncol * WMAX
    span = own + 2 * WMAX
    m = wells.shape[1]
    vmem = pl.BlockSpec(memory_space=pltpu.VMEM)
    out = lambda *s: pltpu.HBM(s, F32)
    return pl.pallas_call(
        functools.partial(prep_kernel, nrow),
        in_specs=[vmem] * 5 + [pl.BlockSpec(memory_space=pltpu.HBM)],
        out_specs=[vmem] * 6,
        out_shape=[
            out(own, cols), out(2 * WMAX, cols), out(own, NGY), out(own, NGY),
            out(WMAX, NGY), out(slots, NGY),
        ],
        scratch_shapes=[
            pltpu.VMEM((center.shape[0], 6 * NGY), F32),
            pltpu.VMEM((slots + 2 * WMAX, NGY), F32),
            pltpu.VMEM((8, span), jnp.int32),
            pltpu.SMEM((8, span), jnp.int32),
            pltpu.VMEM((5, span, NGY), F32),
            pltpu.VMEM((5 * own, cols), F32),
            pltpu.VMEM((2 * WMAX, cols), F32),
            pltpu.SemaphoreType.DMA,
            pltpu.SemaphoreType.DMA,
            pltpu.SemaphoreType.DMA,
        ],
        compiler_params=pltpu.CompilerParams(vmem_limit_bytes=SCOPED),
        name="prep",
    )(wells, noise, center, links, process, cov)


def eliminate(a_ref, dcol, first):
    slots = a_ref.shape[0]
    groups = PANEL // 8
    tiles = slots // NGY
    last = first + PANEL
    sub = lax.broadcasted_iota(jnp.int32, (8, NGY), 0)
    lane = lax.broadcasted_iota(jnp.int32, (8, NGY), 1)
    full = lambda v: jnp.broadcast_to(v, (8, NGY))
    rows = [slice(first + 8 * g, first + 8 * g + 8) for g in range(groups)]
    col, strip, dinv = {}, {}, {}
    for g in range(groups):
        for j in range(8 * g + 8):
            col[g, j] = full(a_ref[rows[g], first + j : first + j + 1])
        for t in range(tiles):
            at = lane + t * NGY
            inside = (at >= first) & (at < last)
            eye = jnp.where(at - first == sub + 8 * g, 1.0, 0.0)
            strip[g, t] = jnp.where(inside, eye, a_ref[rows[g], t * NGY : (t + 1) * NGY])
        dinv[g] = jnp.zeros((8, NGY), F32)
    for k in range(PANEL):
        gk, kk = divmod(k, 8)
        scale = 1.0 / full(col[gk, k][kk : kk + 1])
        dinv[gk] = jnp.where(sub == kk, scale, dinv[gk])
        low = {g: col[g, k] * scale for g in range(gk, groups)}
        low[gk] = jnp.where(sub > kk, low[gk], 0.0)
        for j in range(k + 1, PANEL):
            gj, jj = divmod(j, 8)
            up = full(col[gj, k][jj : jj + 1])
            for g in range(gj, groups):
                col[g, j] = col[g, j] - low[g] * up
        for t in range(tiles):
            row = full(strip[gk, t][kk : kk + 1])
            for g in range(gk, groups):
                strip[g, t] = strip[g, t] - low[g] * row
    u, x = [], []
    for g in range(groups):
        dcol[rows[g], :] = dinv[g]
        u.append(jnp.concatenate([strip[g, t] for t in range(tiles)], axis=1))
        x.append(
            jnp.concatenate(
                [jnp.where(lane + t * NGY >= last, strip[g, t] * dinv[g], 0.0) for t in range(tiles)], axis=1
            )
        )
    u = jnp.concatenate(u, axis=0)
    x = jnp.concatenate(x, axis=0)
    a_ref[first:last, :] = u
    if last < slots:
        base = last // NGY * NGY
        take = coldot(x[:, base:], u)
        at = lax.broadcasted_iota(jnp.int32, (slots - last, slots), 1)
        rest = jnp.where((at >= first) & (at < last), 0.0, a_ref[last:, :])
        a_ref[last:, :] = rest - take[last - base :]


def main_kernel(
    nrow, ncol, pieces,
    cov_ref, bp_ref, sp_ref, ownc_ref, ownp_ref, colc_ref, diag_ref,
    center_ref, links_ref, process_ref,
    pred_ref, across, strip_ref,
    ccol, rowt, xbuf, even, odd, lh, rh, rtop, rbot, rfirst, rlast,
    spin, hl, hr, gz, smat, dcol,
    x_sem, col_send, col_recv, spin_send, spin_recv, edge_send, edge_recv,
    gz_send, gz_recv, s_send, s_recv, ac_send, ac_recv, halo_send, halo_recv,
    ring_send, ring_recv, swap_send, swap_recv,
):
    rows, cols = cov_ref.shape
    rt = rows // NGY
    ct = cols // NGY
    own = bp_ref.shape[0]
    slots = across.shape[0]
    ngx = center_ref.shape[0]
    r = lax.axis_index("row")
    c = lax.axis_index("col")
    up, down = r > 0, r < nrow - 1
    lef, rig = c > 0, c < ncol - 1
    one = lambda cond: jnp.where(cond, 1, 0)

    def remote(src, dst, ssem, rsem, dr, dc):
        return pltpu.make_async_remote_copy(
            src_ref=src, dst_ref=dst, send_sem=ssem, recv_sem=rsem,
            device_id={"row": dr, "col": dc}, device_id_type=MESH,
        )

    base = pl.multiple_of(c * ct, 8)
    lane = lax.broadcasted_iota(jnp.int32, (ct, NGY), 1)
    ccol[0] = center_ref[pl.ds(base, ct), :]
    for t in range(4):
        v = links_ref[pl.ds(pl.multiple_of(t * ngx + base, 8), ct), :]
        if t == 2:
            v = jnp.where(lane == 0, 0.0, v)
        if t == 3:
            v = jnp.where(lane == NGY - 1, 0.0, v)
        ccol[t + 1] = v

    sub = lax.broadcasted_iota(jnp.int32, (NGY, ngx), 0)
    for t in range(5):
        v = (center_ref[...] if t == 0 else links_ref[(t - 1) * ngx : t * ngx, :]).T
        if t == 3:
            v = jnp.where(sub == 0, 0.0, v)
        if t == 4:
            v = jnp.where(sub == NGY - 1, 0.0, v)
        rowt[t] = v

    even[...] = jnp.zeros(even.shape, F32)
    odd[...] = jnp.zeros(odd.shape, F32)

    @pl.when(r == 0)
    def _():
        rtop[...] = jnp.zeros(rtop.shape, F32)
        spin[0] = jnp.zeros(spin.shape[1:], F32)
        hl[1] = jnp.zeros(hl.shape[1:], F32)
        hr[1] = jnp.zeros(hr.shape[1:], F32)

    @pl.when(r == nrow - 1)
    def _():
        rbot[...] = jnp.zeros(rbot.shape, F32)
        spin[1] = jnp.zeros(spin.shape[1:], F32)
        hl[2] = jnp.zeros(hl.shape[1:], F32)
        hr[2] = jnp.zeros(hr.shape[1:], F32)

    @pl.when(c == 0)
    def _():
        lh[...] = jnp.zeros(lh.shape, F32)
        hl[...] = jnp.zeros(hl.shape, F32)

    @pl.when(c == ncol - 1)
    def _():
        rh[...] = jnp.zeros(rh.shape, F32)
        hr[...] = jnp.zeros(hr.shape, F32)

    bar = pltpu.get_barrier_semaphore()

    def greet(dr, dc):
        pl.semaphore_signal(bar, 1, device_id={"row": dr, "col": dc}, device_id_type=MESH)

    for d in range(1, nrow):
        greet(lax.rem(r + d, nrow), c)
    for d in range(1, ncol):
        greet(r, lax.rem(c + d, ncol))
    for dr, okr in ((-1, up), (1, down)):
        for dc, okc in ((-1, lef), (1, rig)):
            @pl.when(okr & okc)
            def _():
                greet(r + dr, c + dc)
    diagonals = (one(up) + one(down)) * (one(lef) + one(rig))
    pl.semaphore_wait(bar, nrow - 1 + ncol - 1 + diagonals)

    half_rows = lambda k: pl.ds(k * WMAX, WMAX)
    small = []

    def exchange(cond_send, cond_recv, src, dst, ssem, rsem, dr, dc):
        copy = remote(src, dst, ssem, rsem, dr, dc)
        pl.when(cond_send)(copy.start)
        small.append((cond_send, cond_recv, copy))

    exchange(up, down, sp_ref.at[half_rows(0)], spin.at[1], spin_send.at[0], spin_recv.at[0], r - 1, c)
    exchange(down, up, sp_ref.at[half_rows(1)], spin.at[0], spin_send.at[1], spin_recv.at[1], r + 1, c)
    for side, ok, no, buf, dc in ((0, lef, rig, hr, -1), (1, rig, lef, hl, 1)):
        at = slice(0, NGY) if side == 0 else slice(cols - NGY, cols)
        exchange(ok, no, bp_ref.at[:, at], buf.at[0], edge_send.at[side, 0], edge_recv.at[side, 0], r, c + dc)
        exchange(
            up & ok, down & no, sp_ref.at[half_rows(0), at], buf.at[2, half_rows(0)],
            edge_send.at[side, 1], edge_recv.at[side, 1], r - 1, c + dc,
        )
        exchange(
            down & ok, up & no, sp_ref.at[half_rows(1), at], buf.at[1, half_rows(0)],
            edge_send.at[side, 2], edge_recv.at[side, 2], r + 1, c + dc,
        )

    cols_out = []
    for n, (t0, tiles) in enumerate(pieces):
        at = pl.ds(t0 * NGY, tiles * NGY)
        to_left = remote(cov_ref.at[at, 0:NGY], rh.at[at], col_send.at[0, n], col_recv.at[0, n], r, c - 1)
        to_right = remote(
            cov_ref.at[at, cols - NGY : cols], lh.at[at], col_send.at[1, n], col_recv.at[1, n], r, c + 1
        )
        cols_out.append((to_left, to_right))

    def start_cols(n):
        if n < len(pieces):
            pl.when(lef)(cols_out[n][0].start)
            pl.when(rig)(cols_out[n][1].start)

    for n in range(3):
        start_cols(n)

    def fetch(t):
        b = lax.rem(t, 3)
        return pltpu.make_async_copy(
            cov_ref.at[pl.ds(pl.multiple_of(t * NGY, NGY), NGY), :], xbuf.at[b], x_sem.at[b]
        )

    fetch(0).start()
    fetch(1).start()

    for cond_send, cond_recv, copy in small:
        pl.when(cond_recv)(copy.wait_recv)

    mine = pl.ds(pl.multiple_of(r * own, own), own)

    def total(k):
        if k < 0:
            main, top, bottom = hl[0], hl[1, 0:WMAX], hl[2, 0:WMAX]
        elif k == ct:
            main, top, bottom = hr[0], hr[1, 0:WMAX], hr[2, 0:WMAX]
        else:
            at = slice(k * NGY, (k + 1) * NGY)
            main, top, bottom = bp_ref[:, at], spin[0, :, at], spin[1, :, at]
        if own == 2 * WMAX:
            return main + jnp.concatenate([top, bottom], axis=0)
        gap = jnp.zeros((own - 2 * WMAX, NGY), F32)
        return main + jnp.concatenate([top, gap, bottom], axis=0)

    cell_at = ownc_ref[...] - (c * cols).astype(F32)
    before, here = total(-1), total(0)
    for k in range(ct):
        after = total(k + 1)
        acc = ccol[0, k : k + 1] * here + ccol[1, k : k + 1] * before + ccol[2, k : k + 1] * after
        acc = acc + ccol[3, k : k + 1] * pltpu.roll(here, 1, 1)
        acc = acc + ccol[4, k : k + 1] * pltpu.roll(here, NGY - 1, 1)
        hit = cell_at == iota((own, NGY), 1) + k * NGY
        acc = acc + jnp.where(hit, ownp_ref[...], 0.0)
        across[mine, k * NGY : (k + 1) * NGY] = acc
        before, here = here, after

    nchip = ncol // 2
    hop = nchip // 2
    chip, core = c // 2, lax.rem(c, 2)

    def place(q):
        return jnp.where(lax.rem(q, 2) == 0, q // 2, nchip - 1 - q // 2)

    def chip_at(pos):
        pos = lax.rem(pos + nchip, nchip)
        return jnp.where(pos < hop, 2 * pos, 2 * (nchip - 1 - pos) + 1)

    pos, src_pos = place(chip), place(r)
    dist = (lax.rem(pos - src_pos + nchip, nchip), lax.rem(src_pos - pos + nchip, nchip))
    nxt = (chip_at(pos + 1) * 2 + core, chip_at(pos - 1) * 2 + core)
    is_src = dist[0] == 0
    count = 2 * nrow
    turns = count + nchip - 1
    share = (own // 4 // 2, own * 3 // 4 // 2)

    def nearest(n):
        table = [sorted(range(nrow), key=lambda z: abs(z - q)) for q in range(nrow)]
        z = 0
        for q in range(nrow):
            for m in range(nrow):
                z = z + jnp.where((r == q) & (n == m), table[q][m], 0)
        return z

    def pass_on(src, dst):
        at = pl.ds(pl.multiple_of(src * own, own), own)
        side = jnp.where(dst > r, 1, 0)
        return remote(across.at[at], across.at[at], ac_send.at[side, src], ac_recv.at[src], dst, c)

    def gather_turn(u):
        @pl.when(r - u >= 0)
        def _():
            copy = pass_on(r - u, r + 1)
            copy.wait_recv()
            pl.when(down)(copy.start)

        @pl.when(r + u < nrow)
        def _():
            copy = pass_on(r + u, r - 1)
            copy.wait_recv()
            pl.when(up)(copy.start)

    def gather_drain():
        for u in range(nrow - 1):
            @pl.when((r - u >= 0) & down)
            def _():
                pass_on(r - u, r + 1).wait_send()

            @pl.when((r + u < nrow) & up)
            def _():
                pass_on(r + u, r - 1).wait_send()

    def moves(n, h):
        z = nearest(n // 2)
        start = z * own + h * 2 * share[0] + lax.rem(n, 2) * share[h]
        at = pl.ds(pl.multiple_of(start, 8), share[h])
        here, there = strip_ref.at[core, at], strip_ref.at[1 - core, at]
        fwd = remote(here, here, ring_send.at[h, n], ring_recv.at[h, n], r, nxt[h])
        swap = remote(here, here, swap_send.at[h, n], swap_recv.at[h, n], r, c + 1 - 2 * core)
        back = remote(there, there, swap_send.at[h, n], swap_recv.at[h, n], r, c + 1 - 2 * core)
        return at, fwd, swap, back

    def relay(t):
        @pl.when((lax.rem(t, 2) == 0) & (t >= 2) & (t < count))
        def _():
            gather_turn(t // 2)

        for h in range(2):
            n = t - dist[h]

            @pl.when((n >= 0) & (n < count))
            def _():
                at, fwd, swap, _ = moves(n, h)

                @pl.when(is_src)
                def _():
                    strip_ref[core, at, :] = across[at, :]

                @pl.when(jnp.logical_not(is_src))
                def _():
                    fwd.wait_recv()

                pl.when(dist[h] < nchip - 1)(fwd.start)
                swap.start()

    pick_at = colc_ref[...] - (c * cols).astype(F32)
    gram = jnp.zeros((WMAX, own), F32)
    for k in range(ct):
        pick = jnp.where(pick_at == iota((WMAX, NGY), 1) + k * NGY, 1.0, 0.0)
        gram = gram + rowdot(pick, across[mine, k * NGY : (k + 1) * NGY])
    gz[r, :, 0:own] = gram

    gz_out = []
    for d in range(1, nrow):
        peer = lax.rem(r + d, nrow)
        copy = remote(gz.at[r], gz.at[r], gz_send.at[d - 1], gz_recv.at[r], peer, c)
        copy.start()
        gz_out.append(copy)
    for d in range(1, nrow):
        src = lax.rem(r + d, nrow)
        remote(gz.at[src], gz.at[src], gz_send.at[0], gz_recv.at[src], src, c).wait_recv()
    pl.when(down)(pass_on(r, r + 1).start)
    pl.when(up)(pass_on(r, r - 1).start)
    srow = pl.ds(pl.multiple_of(c * WMAX, WMAX), WMAX)
    for j in range(nrow):
        smat[srow, j * own : (j + 1) * own] = gz[j, :, 0:own]
    s_out = []
    for d in range(1, ncol):
        peer = lax.rem(c + d, ncol)
        copy = remote(smat.at[srow], smat.at[srow], s_send.at[d - 1], s_recv.at[c], r, peer)
        copy.start()
        s_out.append(copy)
    for d in range(1, ncol):
        src = lax.rem(c + d, ncol)
        at = pl.ds(pl.multiple_of(src * WMAX, WMAX), WMAX)
        remote(smat.at[at], smat.at[at], s_send.at[0], s_recv.at[src], r, src).wait_recv()

    start_cols(3)
    relay(0)

    for copy in s_out:
        copy.wait_send()

    tiles = [slice(k * NGY, (k + 1) * NGY) for k in range(slots // NGY)]
    for at in tiles:
        eye = lax.broadcasted_iota(jnp.int32, (slots, NGY), 0) == (
            lax.broadcasted_iota(jnp.int32, (slots, NGY), 1) + at.start
        )
        smat[:, at] = smat[:, at] + jnp.where(eye, diag_ref[...], 0.0)
    for first in range(0, slots, PANEL):
        eliminate(smat, dcol, first)
        if first == slots // 2:
            relay(1)

    groups = NGY // RG

    def right_group(t, b, g, k, before, here):
        at = pl.ds(pl.multiple_of(g * RG, RG), RG)
        gat = pl.ds(pl.multiple_of(t * NGY + g * RG, RG), RG)
        if k < 0:
            return lh[gat, :], xbuf[b, at, 0:NGY]
        after = xbuf[b, at, (k + 1) * NGY : (k + 2) * NGY] if k < ct - 1 else rh[gat, :]
        acc = ccol[0, k : k + 1] * here + ccol[1, k : k + 1] * before + ccol[2, k : k + 1] * after
        acc = acc + ccol[3, k : k + 1] * pltpu.roll(here, 1, 1)
        acc = acc + ccol[4, k : k + 1] * pltpu.roll(here, NGY - 1, 1)
        return here, after, acc

    def right_apply(t, b, dst, pad):
        def body(g, carry):
            before, here = right_group(t, b, g, -1, None, None)
            for k in range(ct):
                before, here, acc = right_group(t, b, g, k, before, here)
                dst[k, pl.ds(pl.multiple_of(pad + g * RG, 8), RG), :] = acc
            return carry

        lax.fori_loop(0, groups, body, 0)

    def left_apply(i, mid, other, following):
        gx = r * rt + i
        turn = lax.rem(ngx - gx, ngx)
        b = lax.rem(i + 1, 3)

        def body(g, carry):
            s = pl.ds(pl.multiple_of(g * RG, RG), RG)
            c0, c1, c2, c3, c4 = [
                jnp.broadcast_to(pltpu.roll(rowt[t, s], turn, 1)[:, 0:1], (RG, NGY)) for t in range(5)
            ]
            a0 = PAD + g * RG
            same = pl.ds(pl.multiple_of(a0, 8), RG)
            above = pl.ds(a0 - 1, RG)
            below = pl.ds(a0 + 1, RG)
            at = pl.ds(pl.multiple_of(i * NGY + g * RG, RG), RG)
            if following:
                before, here = right_group(i + 1, b, g, -1, None, None)
            for k in range(ct):
                acc = c0 * mid[k, same] + c1 * other[k, same]
                acc = acc + c3 * mid[k, above] + c4 * mid[k, below]
                if following:
                    before, here, nxt_row = right_group(i + 1, b, g, k, before, here)
                    other[k, same] = nxt_row
                    acc = acc + c2 * nxt_row
                pred_ref[at, k * NGY : (k + 1) * NGY] = acc
            return carry

        lax.fori_loop(0, groups, body, 0)

    def add_process(i):
        gx = r * rt + i
        kd = gx - c * ct

        @pl.when((kd >= 0) & (kd < ct))
        def _():
            sub = lax.broadcasted_iota(jnp.int32, (NGY, NGY), 0)
            lan = lax.broadcasted_iota(jnp.int32, (NGY, NGY), 1)
            add = jnp.where(sub == lan, process_ref[pl.ds(gx, 1), :], 0.0)
            rat = pl.ds(pl.multiple_of(i * NGY, NGY), NGY)
            cat = pl.ds(pl.multiple_of(kd * NGY, NGY), NGY)
            pred_ref[rat, cat] = pred_ref[rat, cat] + add

    def wait_cols(n):
        pl.when(rig)(cols_out[n][0].wait_recv)
        pl.when(lef)(cols_out[n][1].wait_recv)

    wait_cols(0)
    wait_cols(1)
    last = pltpu.make_async_copy(cov_ref.at[pl.ds(rows - NGY, NGY), :], xbuf.at[2], x_sem.at[2])
    last.start()
    fetch(0).wait()
    right_apply(0, 0, even, PAD)
    last.wait()
    right_apply(rt - 1, 2, rlast, 0)
    fetch(2).start()

    def save(k, carry):
        rfirst[k] = even[k, PAD : PAD + NGY, :]
        return carry

    lax.fori_loop(0, ct, save, 0)

    send_up = remote(rfirst, rbot, halo_send.at[0], halo_recv.at[0], r - 1, c)
    send_down = remote(
        rlast, rtop, halo_send.at[1], halo_recv.at[1], r + 1, c
    )

    reach = lambda i: jnp.minimum(i * (turns - 3) // (rt - 3), turns - 3)

    def take_turn(t, carry):
        relay(t)
        return carry

    def step(i, mid, other):
        for n in range(2, len(pieces)):
            @pl.when(i + 1 == pieces[n][0])
            def _():
                wait_cols(n)
                start_cols(n + 2)

        @pl.when(i == rt // 2)
        def _():
            pl.when(up)(send_up.start)
            pl.when(down)(send_down.start)

        done = jnp.where(i == 0, 2, reach(i - 1) + 3)
        lax.fori_loop(done, reach(i) + 3, take_turn, 0)
        fetch(i + 1).wait()

        @pl.when(i + 3 < rt)
        def _():
            fetch(i + 3).start()

        left_apply(i, mid, other, True)
        add_process(i)

    def pair(p, carry):
        step(2 * p, even, odd)
        step(2 * p + 1, odd, even)
        return carry

    lax.fori_loop(0, (rt - 2) // 2, pair, 0)
    step(rt - 2, even, odd)
    left_apply(rt - 1, odd, even, False)
    add_process(rt - 1)

    gather_drain()
    at = lax.broadcasted_iota(jnp.int32, (slots, slots), 1)
    low = jnp.where(at <= lax.broadcasted_iota(jnp.int32, (slots, slots), 0), smat[...], 0.0)
    wt = cols // 2 if cols // 2 % NGY == 0 else cols
    for k in range(cols // wt):
        at = slice(k * wt, (k + 1) * wt)
        y = jnp.dot(low, across[:, at], precision=HIGHEST) * dcol[:, 0:1]
        across[:, at] = coldot(low, y)

    pl.when(down)(send_up.wait_recv)
    pl.when(up)(send_down.wait_recv)
    for side, buf, link, t in ((0, rtop, 0, 0), (1, rbot, 1, rt - 1)):
        gx = r * rt + t
        v = jnp.broadcast_to(links_ref[pl.ds(link * ngx + gx, 1), :], (NGY, NGY)).T
        for k in range(ct):
            rat = slice(t * NGY, (t + 1) * NGY)
            cat = slice(k * NGY, (k + 1) * NGY)
            pred_ref[rat, cat] = pred_ref[rat, cat] + v * buf[k]

    def drain(n, carry):
        for h in range(2):
            _, fwd, swap, back = moves(n, h)
            back.wait_recv()
            swap.wait_send()
            pl.when(dist[h] < nchip - 1)(fwd.wait_send)
        return carry

    lax.fori_loop(0, count, drain, 0)
    for copy in gz_out:
        copy.wait_send()
    for cond_send, cond_recv, copy in small:
        pl.when(cond_send)(copy.wait_send)
    for to_left, to_right in cols_out:
        pl.when(lef)(to_left.wait_send)
        pl.when(rig)(to_right.wait_send)
    pl.when(up)(send_up.wait_send)
    pl.when(down)(send_down.wait_send)


def main(nrow, ncol, cov, bp, sp, ownc, ownp, colc, diag, center, links, process):
    rows, cols = cov.shape
    rt, ct = rows // NGY, cols // NGY
    own = bp.shape[0]
    slots = diag.shape[0]
    middle = list(range(1, rt - 1, 5)) + [rt - 1]
    pieces = [(0, 1), (rt - 1, 1)] + [(a, b - a) for a, b in zip(middle, middle[1:])]
    nchunk = len(pieces)
    vmem = pl.BlockSpec(memory_space=pltpu.VMEM)
    dma = lambda *s: pltpu.SemaphoreType.DMA(s)
    return pl.pallas_call(
        functools.partial(main_kernel, nrow, ncol, tuple(pieces)),
        in_specs=[pl.BlockSpec(memory_space=pltpu.HBM)] + [vmem] * 9,
        out_specs=[vmem] * 3,
        out_shape=[
            pltpu.VMEM((rows, cols), F32),
            pltpu.VMEM((slots, cols), F32),
            pltpu.VMEM((2, slots, cols), F32),
        ],
        scratch_shapes=[
            pltpu.VMEM((5, ct, NGY), F32),
            pltpu.VMEM((5, NGY, center.shape[0]), F32),
            pltpu.VMEM((3, NGY, cols), F32),
            pltpu.VMEM((ct, NGY + 2 * PAD, NGY), F32),
            pltpu.VMEM((ct, NGY + 2 * PAD, NGY), F32),
            pltpu.VMEM((rows, NGY), F32),
            pltpu.VMEM((rows, NGY), F32),
            pltpu.VMEM((ct, NGY, NGY), F32),
            pltpu.VMEM((ct, NGY, NGY), F32),
            pltpu.VMEM((ct, NGY, NGY), F32),
            pltpu.VMEM((ct, NGY, NGY), F32),
            pltpu.VMEM((2, WMAX, cols), F32),
            pltpu.VMEM((3, own, NGY), F32),
            pltpu.VMEM((3, own, NGY), F32),
            pltpu.VMEM((nrow, WMAX, NGY), F32),
            pltpu.VMEM((slots, slots), F32),
            pltpu.VMEM((slots, NGY), F32),
            dma(3), dma(2, nchunk), dma(2, nchunk), dma(2), dma(2), dma(2, 3), dma(2, 3),
            dma(nrow), dma(nrow), dma(ncol), dma(ncol), dma(2, nrow), dma(nrow), dma(2), dma(2),
            dma(2, 2 * nrow), dma(2, 2 * nrow), dma(2, 2 * nrow), dma(2, 2 * nrow),
        ],
        compiler_params=pltpu.CompilerParams(
            collective_id=0, has_side_effects=True, vmem_limit_bytes=SCOPED
        ),
        name="main",
    )(cov, bp, sp, ownc, ownp, colc, diag, center, links, process)


def final_kernel(pred_ref, w_ref, strip_ref, o_ref, whi, wlo):
    i = pl.program_id(0)
    tile = o_ref.shape[0]
    cols = o_ref.shape[1]

    @pl.when(i == 0)
    def _():
        hi = w_ref[...].astype(BF16)
        whi[...] = hi
        wlo[...] = (w_ref[...] - hi.astype(F32)).astype(BF16)

    part = cols // tile
    at = pl.ds(pl.multiple_of(lax.rem(i, part) * tile, tile), tile)
    s = strip_ref[i // part, :, at].T
    hi = s.astype(BF16)
    lo = (s - hi.astype(F32)).astype(BF16)
    dot = functools.partial(jnp.dot, preferred_element_type=F32)
    update = dot(hi, whi[...]) + (dot(lo, whi[...]) + dot(hi, wlo[...]))
    o_ref[...] = pred_ref[pl.ds(pl.multiple_of(i * tile, tile), tile), :] - update


def final(pred, w, strip):
    rows, cols = pred.shape
    tile = 256
    vmem = pl.BlockSpec(memory_space=pltpu.VMEM)
    return pl.pallas_call(
        final_kernel,
        grid=(rows // tile,),
        in_specs=[vmem] * 3,
        out_specs=pl.BlockSpec((tile, cols), lambda i: (i, 0)),
        out_shape=jax.ShapeDtypeStruct((rows, cols), F32),
        scratch_shapes=[pltpu.VMEM(w.shape, BF16), pltpu.VMEM(w.shape, BF16)],
        compiler_params=pltpu.CompilerParams(vmem_limit_bytes=SCOPED),
        name="final",
    )(keep(pred), keep(w), keep(strip))


def solution(mesh):
    nrow, ncol = mesh.shape["row"], mesh.shape["col"]

    def shards(covariance, center, links, process, wells, noise):
        center = center.reshape(-1, NGY)
        links = links.reshape(-1, NGY)
        process = process.reshape(-1, NGY)
        small = prep(nrow, ncol, wells, noise, center, links, process, covariance)
        return final(*main(nrow, ncol, covariance, *small, center, links, process))

    in_specs = (P("row", "col"), P(), P(), P(), P(), P())
    out_specs = P("row", "col")
    return jax.shard_map(shards, mesh=mesh, in_specs=in_specs, out_specs=out_specs, check_vma=False)
```

```python
import functools

import jax
import jax.numpy as jnp
from jax import lax
from jax.experimental import pallas as pl
from jax.experimental.pallas import tpu as pltpu
from jax.sharding import PartitionSpec as P

NGY = 128
WMAX = 32
PANEL = 32
PAD = 8
RG = 16
SCOPED = 24 * 2**20
HIGHEST = lax.Precision.HIGHEST
F32 = jnp.float32
BF16 = jnp.bfloat16
MESH = pl.DeviceIdType.MESH


def iota(shape, dim):
    return lax.broadcasted_iota(jnp.int32, shape, dim).astype(F32)


def rowdot(a, b, precision=HIGHEST):
    return lax.dot_general(
        a, b, (((1,), (1,)), ((), ())), precision=precision, preferred_element_type=F32
    )


def coldot(a, b, precision=HIGHEST):
    return lax.dot_general(
        a, b, (((0,), (0,)), ((), ())), precision=precision, preferred_element_type=F32
    )


def prep_kernel(
    nrow, wells_hbm, noise_hbm, center_hbm, links_hbm, process_hbm, cov_ref,
    bp_ref, sp_ref, ownc_ref, ownp_ref, colc_ref, diag_ref, table_ref,
    wells_ref, noise_ref, center_ref, links_ref, process_ref, in_sem, tables, cells, rows_v, rows_s, coef, near, spill, idx_sem, near_sem, spill_sem,
):
    rows, cols = cov_ref.shape
    sources = (wells_hbm, noise_hbm, center_hbm, links_hbm, process_hbm)
    inputs = (wells_ref, noise_ref, center_ref, links_ref, process_ref)
    loads = [pltpu.make_async_copy(a, b, in_sem.at[n]) for n, (a, b) in enumerate(zip(sources, inputs))]
    for load in loads:
        load.start()
    for load in loads[:2]:
        load.wait()
    m = wells_ref.shape[1]
    slots = diag_ref.shape[0]
    ngx = center_ref.shape[0]
    own = bp_ref.shape[0]
    span = own + 2 * WMAX
    r = lax.axis_index("row")
    c = lax.axis_index("col")

    w = wells_ref[...].astype(F32)
    block = jnp.floor(w * (1.0 / cols))
    square = jnp.broadcast_to(block, (m, m)).T
    earlier = (square == block) & (iota((m, m), 0) < iota((m, m), 1))
    rank = jnp.sum(jnp.where(earlier, 1.0, 0.0), axis=0, keepdims=True)
    slot = block * WMAX + rank
    onehot = slot == iota((slots, m), 0)
    cell = jnp.sum(jnp.where(onehot, w + 1.0, 0.0), axis=1, keepdims=True) - 1.0
    noise = jnp.sum(jnp.where(onehot, noise_ref[...], 0.0), axis=1, keepdims=True)
    diag_ref[...] = jnp.broadcast_to(jnp.where(cell < 0.0, 1.0, noise), diag_ref.shape)
    cells[...] = jnp.full(cells.shape, -1.0, F32)
    cells[WMAX : WMAX + slots, :] = jnp.broadcast_to(cell, (slots, NGY))

    mine = cells[pl.ds(pl.multiple_of(r * own, WMAX), span), :]
    colc_ref[...] = cells[pl.ds(pl.multiple_of(WMAX + c * WMAX, WMAX), WMAX), :]
    ownc_ref[...] = mine[WMAX : WMAX + own]
    local = mine - (r * rows).astype(F32)
    rows_v[...] = local.T[0:8].astype(jnp.int32)
    copy = pltpu.make_async_copy(rows_v, rows_s, idx_sem)
    copy.start()

    for load in loads[2:]:
        load.wait()
    tables[:, 0:NGY] = center_ref[...]
    for g in range(ngx):
        for t in range(4):
            tables[g : g + 1, (t + 1) * NGY : (t + 2) * NGY] = links_ref[t : t + 1, g * NGY : (g + 1) * NGY]
    tables[:, 5 * NGY :] = process_ref[...]
    for t in range(6):
        table_ref[t] = tables[:, t * NGY : (t + 1) * NGY]
    gx = jnp.floor(mine[:, :1] * (1.0 / NGY))
    gy = mine[:, :1] - gx * NGY
    pickx = jnp.where(gx == iota((span, ngx), 1), 1.0, 0.0)
    table = jnp.dot(pickx, tables[...], precision=HIGHEST)
    copy.wait()

    moves = (0, -NGY, NGY, -1, 1)

    def row(i):
        return cov_ref.at[pl.ds(jnp.clip(i, 0, rows - 1), 1), :]

    def gather(i, carry):
        at = rows_s[0, WMAX + i]
        for t in range(5):
            dst = near.at[pl.ds(t * own + i, 1), :]
            pltpu.make_async_copy(row(at + moves[t]), dst, near_sem).start()
        return carry

    lax.fori_loop(0, own, gather, 0)

    def gather_spill(i, carry):
        low = spill.at[pl.ds(i, 1), :]
        high = spill.at[pl.ds(WMAX + i, 1), :]
        pltpu.make_async_copy(row(rows_s[0, i] + NGY), low, spill_sem).start()
        pltpu.make_async_copy(row(rows_s[0, WMAX + own + i] - NGY), high, spill_sem).start()
        return carry

    lax.fori_loop(0, WMAX, gather_spill, 0)

    picky = gy == iota((span, NGY), 1)
    valid = mine[:, :1] >= 0.0
    lv = local[:, :1]
    for t in range(5):
        value = jnp.sum(
            jnp.where(picky, table[:, t * NGY : (t + 1) * NGY], 0.0), axis=1, keepdims=True
        )
        target = lv + moves[t]
        ok = valid & (target >= 0.0) & (target < rows)
        if t == 3:
            ok = ok & (gy > 0.0)
        if t == 4:
            ok = ok & (gy < NGY - 1.0)
        coef[t] = jnp.broadcast_to(jnp.where(ok, value, 0.0), (span, NGY))
    value = jnp.sum(jnp.where(picky, table[:, 5 * NGY :], 0.0), axis=1, keepdims=True)
    value = jnp.where(valid, value, 0.0)
    ownp_ref[...] = jnp.broadcast_to(value[WMAX : WMAX + own], (own, NGY))

    pltpu.make_async_copy(cov_ref.at[pl.ds(0, 5 * own), :], near, near_sem).wait()
    pltpu.make_async_copy(cov_ref.at[pl.ds(0, 2 * WMAX), :], spill, spill_sem).wait()
    for k in range(cols // NGY):
        at = slice(k * NGY, (k + 1) * NGY)
        acc = coef[0, WMAX : WMAX + own] * near[0:own, at]
        for t in range(1, 5):
            acc = acc + coef[t, WMAX : WMAX + own] * near[t * own : (t + 1) * own, at]
        bp_ref[:, at] = acc
        sp_ref[:WMAX, at] = coef[2, :WMAX] * spill[:WMAX, at]
        sp_ref[WMAX:, at] = coef[1, WMAX + own :] * spill[WMAX:, at]


def keep(a):
    return pltpu.with_memory_space_constraint(a, pltpu.VMEM)


def prep(nrow, ncol, wells, noise, center, links, process, cov):
    rows, cols = cov.shape
    ratio = rows // cols
    own = ratio * WMAX
    slots = ncol * WMAX
    span = own + 2 * WMAX
    m = wells.shape[1]
    vmem = pl.BlockSpec(memory_space=pltpu.VMEM)
    out = lambda *s: pltpu.HBM(s, F32)
    return pl.pallas_call(
        functools.partial(prep_kernel, nrow),
        in_specs=[pl.BlockSpec(memory_space=pltpu.HBM)] * 6,
        out_specs=[vmem] * 7,
        out_shape=[
            out(own, cols), out(2 * WMAX, cols), out(own, NGY), out(own, NGY),
            out(WMAX, NGY), out(slots, NGY), out(6, center.shape[0], NGY),
        ],
        scratch_shapes=[
            pltpu.VMEM(wells.shape, jnp.int32),
            pltpu.VMEM(noise.shape, F32),
            pltpu.VMEM(center.shape, F32),
            pltpu.VMEM(links.shape, F32),
            pltpu.VMEM(process.shape, F32),
            pltpu.SemaphoreType.DMA((5,)),
            pltpu.VMEM((center.shape[0], 6 * NGY), F32),
            pltpu.VMEM((slots + 2 * WMAX, NGY), F32),
            pltpu.VMEM((8, span), jnp.int32),
            pltpu.SMEM((8, span), jnp.int32),
            pltpu.VMEM((5, span, NGY), F32),
            pltpu.VMEM((5 * own, cols), F32),
            pltpu.VMEM((2 * WMAX, cols), F32),
            pltpu.SemaphoreType.DMA,
            pltpu.SemaphoreType.DMA,
            pltpu.SemaphoreType.DMA,
        ],
        compiler_params=pltpu.CompilerParams(vmem_limit_bytes=SCOPED),
        name="prep",
    )(*[pltpu.with_memory_space_constraint(a, pltpu.HBM) for a in (wells, noise, center, links, process)], cov)


def eliminate(a_ref, dcol, first):
    slots = a_ref.shape[0]
    groups = PANEL // 8
    tiles = slots // NGY
    last = first + PANEL
    sub = lax.broadcasted_iota(jnp.int32, (8, NGY), 0)
    lane = lax.broadcasted_iota(jnp.int32, (8, NGY), 1)
    full = lambda v: jnp.broadcast_to(v, (8, NGY))
    rows = [slice(first + 8 * g, first + 8 * g + 8) for g in range(groups)]
    col, strip, dinv = {}, {}, {}
    for g in range(groups):
        for j in range(8 * g + 8):
            col[g, j] = full(a_ref[rows[g], first + j : first + j + 1])
        for t in range(tiles):
            at = lane + t * NGY
            inside = (at >= first) & (at < last)
            eye = jnp.where(at - first == sub + 8 * g, 1.0, 0.0)
            strip[g, t] = jnp.where(inside, eye, a_ref[rows[g], t * NGY : (t + 1) * NGY])
        dinv[g] = jnp.zeros((8, NGY), F32)
    for k in range(PANEL):
        gk, kk = divmod(k, 8)
        scale = 1.0 / full(col[gk, k][kk : kk + 1])
        dinv[gk] = jnp.where(sub == kk, scale, dinv[gk])
        low = {g: col[g, k] * scale for g in range(gk, groups)}
        low[gk] = jnp.where(sub > kk, low[gk], 0.0)
        for j in range(k + 1, PANEL):
            gj, jj = divmod(j, 8)
            up = full(col[gj, k][jj : jj + 1])
            for g in range(gj, groups):
                col[g, j] = col[g, j] - low[g] * up
        for t in range(tiles):
            row = full(strip[gk, t][kk : kk + 1])
            for g in range(gk, groups):
                strip[g, t] = strip[g, t] - low[g] * row
    u, x = [], []
    for g in range(groups):
        dcol[rows[g], :] = dinv[g]
        u.append(jnp.concatenate([strip[g, t] for t in range(tiles)], axis=1))
        x.append(
            jnp.concatenate(
                [jnp.where(lane + t * NGY >= last, strip[g, t] * dinv[g], 0.0) for t in range(tiles)], axis=1
            )
        )
    u = jnp.concatenate(u, axis=0)
    x = jnp.concatenate(x, axis=0)
    a_ref[first:last, :] = u
    if last < slots:
        base = last // NGY * NGY
        take = coldot(x[:, base:], u)
        at = lax.broadcasted_iota(jnp.int32, (slots - last, slots), 1)
        rest = jnp.where((at >= first) & (at < last), 0.0, a_ref[last:, :])
        a_ref[last:, :] = rest - take[last - base :]


def main_kernel(
    nrow, ncol, pieces,
    cov_ref, bp_ref, sp_ref, ownc_ref, ownp_ref, colc_ref, diag_ref,
    table_ref,
    pred_ref, across, strip_ref,
    ccol, rowt, xbuf, even, odd, lh, rh, rtop, rbot, rfirst, rlast,
    spin, hl, hr, gz, smat, dcol,
    x_sem, col_send, col_recv, spin_send, spin_recv, edge_send, edge_recv,
    gz_send, gz_recv, s_send, s_recv, ac_send, ac_recv, halo_send, halo_recv,
    ring_send, ring_recv, swap_send, swap_recv,
):
    rows, cols = cov_ref.shape
    rt = rows // NGY
    ct = cols // NGY
    own = bp_ref.shape[0]
    slots = across.shape[0]
    ngx = table_ref.shape[1]
    r = lax.axis_index("row")
    c = lax.axis_index("col")
    up, down = r > 0, r < nrow - 1
    lef, rig = c > 0, c < ncol - 1
    one = lambda cond: jnp.where(cond, 1, 0)

    def remote(src, dst, ssem, rsem, dr, dc):
        return pltpu.make_async_remote_copy(
            src_ref=src, dst_ref=dst, send_sem=ssem, recv_sem=rsem,
            device_id={"row": dr, "col": dc}, device_id_type=MESH,
        )

    base = pl.multiple_of(c * ct, 8)
    lane = lax.broadcasted_iota(jnp.int32, (ct, NGY), 1)
    for t in range(5):
        v = table_ref[t, pl.ds(base, ct), :]
        if t == 3:
            v = jnp.where(lane == 0, 0.0, v)
        if t == 4:
            v = jnp.where(lane == NGY - 1, 0.0, v)
        ccol[t] = v

    sub = lax.broadcasted_iota(jnp.int32, (NGY, ngx), 0)
    for t in range(5):
        v = table_ref[t].T
        if t == 3:
            v = jnp.where(sub == 0, 0.0, v)
        if t == 4:
            v = jnp.where(sub == NGY - 1, 0.0, v)
        rowt[t] = v

    even[...] = jnp.zeros(even.shape, F32)
    odd[...] = jnp.zeros(odd.shape, F32)

    @pl.when(r == 0)
    def _():
        rtop[...] = jnp.zeros(rtop.shape, F32)
        spin[0] = jnp.zeros(spin.shape[1:], F32)
        hl[1] = jnp.zeros(hl.shape[1:], F32)
        hr[1] = jnp.zeros(hr.shape[1:], F32)

    @pl.when(r == nrow - 1)
    def _():
        rbot[...] = jnp.zeros(rbot.shape, F32)
        spin[1] = jnp.zeros(spin.shape[1:], F32)
        hl[2] = jnp.zeros(hl.shape[1:], F32)
        hr[2] = jnp.zeros(hr.shape[1:], F32)

    @pl.when(c == 0)
    def _():
        lh[...] = jnp.zeros(lh.shape, F32)
        hl[...] = jnp.zeros(hl.shape, F32)

    @pl.when(c == ncol - 1)
    def _():
        rh[...] = jnp.zeros(rh.shape, F32)
        hr[...] = jnp.zeros(hr.shape, F32)

    bar = pltpu.get_barrier_semaphore()

    def greet(dr, dc):
        pl.semaphore_signal(bar, 1, device_id={"row": dr, "col": dc}, device_id_type=MESH)

    for d in range(1, nrow):
        greet(lax.rem(r + d, nrow), c)
    for d in range(1, ncol):
        greet(r, lax.rem(c + d, ncol))
    for dr, okr in ((-1, up), (1, down)):
        for dc, okc in ((-1, lef), (1, rig)):
            @pl.when(okr & okc)
            def _():
                greet(r + dr, c + dc)
    diagonals = (one(up) + one(down)) * (one(lef) + one(rig))
    pl.semaphore_wait(bar, nrow - 1 + ncol - 1 + diagonals)

    half_rows = lambda k: pl.ds(k * WMAX, WMAX)
    small = []

    def exchange(cond_send, cond_recv, src, dst, ssem, rsem, dr, dc):
        copy = remote(src, dst, ssem, rsem, dr, dc)
        pl.when(cond_send)(copy.start)
        small.append((cond_send, cond_recv, copy))

    exchange(up, down, sp_ref.at[half_rows(0)], spin.at[1], spin_send.at[0], spin_recv.at[0], r - 1, c)
    exchange(down, up, sp_ref.at[half_rows(1)], spin.at[0], spin_send.at[1], spin_recv.at[1], r + 1, c)
    for side, ok, no, buf, dc in ((0, lef, rig, hr, -1), (1, rig, lef, hl, 1)):
        at = slice(0, NGY) if side == 0 else slice(cols - NGY, cols)
        exchange(ok, no, bp_ref.at[:, at], buf.at[0], edge_send.at[side, 0], edge_recv.at[side, 0], r, c + dc)
        exchange(
            up & ok, down & no, sp_ref.at[half_rows(0), at], buf.at[2, half_rows(0)],
            edge_send.at[side, 1], edge_recv.at[side, 1], r - 1, c + dc,
        )
        exchange(
            down & ok, up & no, sp_ref.at[half_rows(1), at], buf.at[1, half_rows(0)],
            edge_send.at[side, 2], edge_recv.at[side, 2], r + 1, c + dc,
        )

    cols_out = []
    for n, (t0, tiles) in enumerate(pieces):
        at = pl.ds(t0 * NGY, tiles * NGY)
        to_left = remote(cov_ref.at[at, 0:NGY], rh.at[at], col_send.at[0, n], col_recv.at[0, n], r, c - 1)
        to_right = remote(
            cov_ref.at[at, cols - NGY : cols], lh.at[at], col_send.at[1, n], col_recv.at[1, n], r, c + 1
        )
        cols_out.append((to_left, to_right))

    def start_cols(n):
        if n < len(pieces):
            pl.when(lef)(cols_out[n][0].start)
            pl.when(rig)(cols_out[n][1].start)

    for n in range(3):
        start_cols(n)

    def fetch(t):
        b = lax.rem(t, 3)
        return pltpu.make_async_copy(
            cov_ref.at[pl.ds(pl.multiple_of(t * NGY, NGY), NGY), :], xbuf.at[b], x_sem.at[b]
        )

    fetch(0).start()
    fetch(1).start()

    for cond_send, cond_recv, copy in small:
        pl.when(cond_recv)(copy.wait_recv)

    mine = pl.ds(pl.multiple_of(r * own, own), own)

    def total(k):
        if k < 0:
            main, top, bottom = hl[0], hl[1, 0:WMAX], hl[2, 0:WMAX]
        elif k == ct:
            main, top, bottom = hr[0], hr[1, 0:WMAX], hr[2, 0:WMAX]
        else:
            at = slice(k * NGY, (k + 1) * NGY)
            main, top, bottom = bp_ref[:, at], spin[0, :, at], spin[1, :, at]
        if own == 2 * WMAX:
            return main + jnp.concatenate([top, bottom], axis=0)
        gap = jnp.zeros((own - 2 * WMAX, NGY), F32)
        return main + jnp.concatenate([top, gap, bottom], axis=0)

    cell_at = ownc_ref[...] - (c * cols).astype(F32)
    before, here = total(-1), total(0)
    for k in range(ct):
        after = total(k + 1)
        acc = ccol[0, k : k + 1] * here + ccol[1, k : k + 1] * before + ccol[2, k : k + 1] * after
        acc = acc + ccol[3, k : k + 1] * pltpu.roll(here, 1, 1)
        acc = acc + ccol[4, k : k + 1] * pltpu.roll(here, NGY - 1, 1)
        hit = cell_at == iota((own, NGY), 1) + k * NGY
        acc = acc + jnp.where(hit, ownp_ref[...], 0.0)
        across[mine, k * NGY : (k + 1) * NGY] = acc
        before, here = here, after

    nchip = ncol // 2
    hop = nchip // 2
    chip, core = c // 2, lax.rem(c, 2)

    def place(q):
        return jnp.where(lax.rem(q, 2) == 0, q // 2, nchip - 1 - q // 2)

    def chip_at(pos):
        pos = lax.rem(pos + nchip, nchip)
        return jnp.where(pos < hop, 2 * pos, 2 * (nchip - 1 - pos) + 1)

    pos, src_pos = place(chip), place(r)
    dist = (lax.rem(pos - src_pos + nchip, nchip), lax.rem(src_pos - pos + nchip, nchip))
    nxt = (chip_at(pos + 1) * 2 + core, chip_at(pos - 1) * 2 + core)
    is_src = dist[0] == 0
    count = 2 * nrow
    turns = count + nchip - 1
    share = (own // 4 // 2, own * 3 // 4 // 2)

    def nearest(n):
        table = [sorted(range(nrow), key=lambda z: abs(z - q)) for q in range(nrow)]
        z = 0
        for q in range(nrow):
            for m in range(nrow):
                z = z + jnp.where((r == q) & (n == m), table[q][m], 0)
        return z

    def pass_on(src, dst):
        at = pl.ds(pl.multiple_of(src * own, own), own)
        side = jnp.where(dst > r, 1, 0)
        return remote(across.at[at], across.at[at], ac_send.at[side, src], ac_recv.at[src], dst, c)

    def gather_turn(u):
        @pl.when(r - u >= 0)
        def _():
            copy = pass_on(r - u, r + 1)
            copy.wait_recv()
            pl.when(down)(copy.start)

        @pl.when(r + u < nrow)
        def _():
            copy = pass_on(r + u, r - 1)
            copy.wait_recv()
            pl.when(up)(copy.start)

    def gather_drain():
        for u in range(nrow - 1):
            @pl.when((r - u >= 0) & down)
            def _():
                pass_on(r - u, r + 1).wait_send()

            @pl.when((r + u < nrow) & up)
            def _():
                pass_on(r + u, r - 1).wait_send()

    def moves(n, h):
        z = nearest(n // 2)
        start = z * own + h * 2 * share[0] + lax.rem(n, 2) * share[h]
        at = pl.ds(pl.multiple_of(start, 8), share[h])
        here, there = strip_ref.at[core, at], strip_ref.at[1 - core, at]
        fwd = remote(here, here, ring_send.at[h, n], ring_recv.at[h, n], r, nxt[h])
        swap = remote(here, here, swap_send.at[h, n], swap_recv.at[h, n], r, c + 1 - 2 * core)
        back = remote(there, there, swap_send.at[h, n], swap_recv.at[h, n], r, c + 1 - 2 * core)
        return at, fwd, swap, back

    def relay(t):
        @pl.when((lax.rem(t, 2) == 0) & (t >= 2) & (t < count))
        def _():
            gather_turn(t // 2)

        for h in range(2):
            n = t - dist[h]

            @pl.when((n >= 0) & (n < count))
            def _():
                at, fwd, swap, _ = moves(n, h)

                @pl.when(is_src)
                def _():
                    strip_ref[core, at, :] = across[at, :]

                @pl.when(jnp.logical_not(is_src))
                def _():
                    fwd.wait_recv()

                pl.when(dist[h] < nchip - 1)(fwd.start)
                swap.start()

    pick_at = colc_ref[...] - (c * cols).astype(F32)
    gram = jnp.zeros((WMAX, own), F32)
    for k in range(ct):
        pick = jnp.where(pick_at == iota((WMAX, NGY), 1) + k * NGY, 1.0, 0.0)
        gram = gram + rowdot(pick, across[mine, k * NGY : (k + 1) * NGY])
    gz[r, :, 0:own] = gram

    gz_out = []
    for d in range(1, nrow):
        peer = lax.rem(r + d, nrow)
        copy = remote(gz.at[r], gz.at[r], gz_send.at[d - 1], gz_recv.at[r], peer, c)
        copy.start()
        gz_out.append(copy)
    for d in range(1, nrow):
        src = lax.rem(r + d, nrow)
        remote(gz.at[src], gz.at[src], gz_send.at[0], gz_recv.at[src], src, c).wait_recv()
    pl.when(down)(pass_on(r, r + 1).start)
    pl.when(up)(pass_on(r, r - 1).start)
    srow = pl.ds(pl.multiple_of(c * WMAX, WMAX), WMAX)
    for j in range(nrow):
        smat[srow, j * own : (j + 1) * own] = gz[j, :, 0:own]
    s_out = []
    for d in range(1, ncol):
        peer = lax.rem(c + d, ncol)
        copy = remote(smat.at[srow], smat.at[srow], s_send.at[d - 1], s_recv.at[c], r, peer)
        copy.start()
        s_out.append(copy)
    for d in range(1, ncol):
        src = lax.rem(c + d, ncol)
        at = pl.ds(pl.multiple_of(src * WMAX, WMAX), WMAX)
        remote(smat.at[at], smat.at[at], s_send.at[0], s_recv.at[src], r, src).wait_recv()

    start_cols(3)
    relay(0)

    for copy in s_out:
        copy.wait_send()

    tiles = [slice(k * NGY, (k + 1) * NGY) for k in range(slots // NGY)]
    for at in tiles:
        eye = lax.broadcasted_iota(jnp.int32, (slots, NGY), 0) == (
            lax.broadcasted_iota(jnp.int32, (slots, NGY), 1) + at.start
        )
        smat[:, at] = smat[:, at] + jnp.where(eye, diag_ref[...], 0.0)
    for first in range(0, slots, PANEL):
        eliminate(smat, dcol, first)
        if first == slots // 2:
            relay(1)

    groups = NGY // RG

    def right_group(t, b, g, k, before, here):
        at = pl.ds(pl.multiple_of(g * RG, RG), RG)
        gat = pl.ds(pl.multiple_of(t * NGY + g * RG, RG), RG)
        if k < 0:
            return lh[gat, :], xbuf[b, at, 0:NGY]
        after = xbuf[b, at, (k + 1) * NGY : (k + 2) * NGY] if k < ct - 1 else rh[gat, :]
        acc = ccol[0, k : k + 1] * here + ccol[1, k : k + 1] * before + ccol[2, k : k + 1] * after
        acc = acc + ccol[3, k : k + 1] * pltpu.roll(here, 1, 1)
        acc = acc + ccol[4, k : k + 1] * pltpu.roll(here, NGY - 1, 1)
        return here, after, acc

    def right_apply(t, b, dst, pad):
        def body(g, carry):
            before, here = right_group(t, b, g, -1, None, None)
            for k in range(ct):
                before, here, acc = right_group(t, b, g, k, before, here)
                dst[k, pl.ds(pl.multiple_of(pad + g * RG, 8), RG), :] = acc
            return carry

        lax.fori_loop(0, groups, body, 0)

    def left_apply(i, mid, other, following):
        gx = r * rt + i
        turn = lax.rem(ngx - gx, ngx)
        b = lax.rem(i + 1, 3)

        def body(g, carry):
            s = pl.ds(pl.multiple_of(g * RG, RG), RG)
            c0, c1, c2, c3, c4 = [
                jnp.broadcast_to(pltpu.roll(rowt[t, s], turn, 1)[:, 0:1], (RG, NGY)) for t in range(5)
            ]
            a0 = PAD + g * RG
            same = pl.ds(pl.multiple_of(a0, 8), RG)
            above = pl.ds(a0 - 1, RG)
            below = pl.ds(a0 + 1, RG)
            at = pl.ds(pl.multiple_of(i * NGY + g * RG, RG), RG)
            if following:
                before, here = right_group(i + 1, b, g, -1, None, None)
            for k in range(ct):
                acc = c0 * mid[k, same] + c1 * other[k, same]
                acc = acc + c3 * mid[k, above] + c4 * mid[k, below]
                if following:
                    before, here, nxt_row = right_group(i + 1, b, g, k, before, here)
                    other[k, same] = nxt_row
                    acc = acc + c2 * nxt_row
                pred_ref[at, k * NGY : (k + 1) * NGY] = acc
            return carry

        lax.fori_loop(0, groups, body, 0)

    def add_process(i):
        gx = r * rt + i
        kd = gx - c * ct

        @pl.when((kd >= 0) & (kd < ct))
        def _():
            sub = lax.broadcasted_iota(jnp.int32, (NGY, NGY), 0)
            lan = lax.broadcasted_iota(jnp.int32, (NGY, NGY), 1)
            add = jnp.where(sub == lan, table_ref[5, pl.ds(gx, 1), :], 0.0)
            rat = pl.ds(pl.multiple_of(i * NGY, NGY), NGY)
            cat = pl.ds(pl.multiple_of(kd * NGY, NGY), NGY)
            pred_ref[rat, cat] = pred_ref[rat, cat] + add

    def wait_cols(n):
        pl.when(rig)(cols_out[n][0].wait_recv)
        pl.when(lef)(cols_out[n][1].wait_recv)

    wait_cols(0)
    wait_cols(1)
    last = pltpu.make_async_copy(cov_ref.at[pl.ds(rows - NGY, NGY), :], xbuf.at[2], x_sem.at[2])
    last.start()
    fetch(0).wait()
    right_apply(0, 0, even, PAD)
    last.wait()
    right_apply(rt - 1, 2, rlast, 0)
    fetch(2).start()

    def save(k, carry):
        rfirst[k] = even[k, PAD : PAD + NGY, :]
        return carry

    lax.fori_loop(0, ct, save, 0)

    send_up = remote(rfirst, rbot, halo_send.at[0], halo_recv.at[0], r - 1, c)
    send_down = remote(
        rlast, rtop, halo_send.at[1], halo_recv.at[1], r + 1, c
    )

    reach = lambda i: jnp.minimum(i * (turns - 3) // (rt - 3), turns - 3)

    def take_turn(t, carry):
        relay(t)
        return carry

    def step(i, mid, other):
        for n in range(2, len(pieces)):
            @pl.when(i + 1 == pieces[n][0])
            def _():
                wait_cols(n)
                start_cols(n + 2)

        @pl.when(i == rt // 2)
        def _():
            pl.when(up)(send_up.start)
            pl.when(down)(send_down.start)

        done = jnp.where(i == 0, 2, reach(i - 1) + 3)
        lax.fori_loop(done, reach(i) + 3, take_turn, 0)
        fetch(i + 1).wait()

        @pl.when(i + 3 < rt)
        def _():
            fetch(i + 3).start()

        left_apply(i, mid, other, True)
        add_process(i)

    def pair(p, carry):
        step(2 * p, even, odd)
        step(2 * p + 1, odd, even)
        return carry

    lax.fori_loop(0, (rt - 2) // 2, pair, 0)
    step(rt - 2, even, odd)
    left_apply(rt - 1, odd, even, False)
    add_process(rt - 1)

    gather_drain()
    at = lax.broadcasted_iota(jnp.int32, (slots, slots), 1)
    low = jnp.where(at <= lax.broadcasted_iota(jnp.int32, (slots, slots), 0), smat[...], 0.0)
    inverse = coldot(low, low * dcol[:, 0:1])
    wt = cols // 2 if cols // 2 % NGY == 0 else cols
    for k in range(cols // wt):
        at = slice(k * wt, (k + 1) * wt)
        across[:, at] = jnp.dot(inverse, across[:, at], precision=HIGHEST)

    pl.when(down)(send_up.wait_recv)
    pl.when(up)(send_down.wait_recv)
    for side, buf, link, t in ((0, rtop, 0, 0), (1, rbot, 1, rt - 1)):
        gx = r * rt + t
        v = jnp.broadcast_to(table_ref[1 + link, pl.ds(gx, 1), :], (NGY, NGY)).T
        for k in range(ct):
            rat = slice(t * NGY, (t + 1) * NGY)
            cat = slice(k * NGY, (k + 1) * NGY)
            pred_ref[rat, cat] = pred_ref[rat, cat] + v * buf[k]

    def drain(n, carry):
        for h in range(2):
            _, fwd, swap, back = moves(n, h)
            back.wait_recv()
            swap.wait_send()
            pl.when(dist[h] < nchip - 1)(fwd.wait_send)
        return carry

    lax.fori_loop(0, count, drain, 0)
    for copy in gz_out:
        copy.wait_send()
    for cond_send, cond_recv, copy in small:
        pl.when(cond_send)(copy.wait_send)
    for to_left, to_right in cols_out:
        pl.when(lef)(to_left.wait_send)
        pl.when(rig)(to_right.wait_send)
    pl.when(up)(send_up.wait_send)
    pl.when(down)(send_down.wait_send)


def main(nrow, ncol, cov, bp, sp, ownc, ownp, colc, diag, table):
    rows, cols = cov.shape
    rt, ct = rows // NGY, cols // NGY
    own = bp.shape[0]
    slots = diag.shape[0]
    middle = list(range(1, rt - 1, 5)) + [rt - 1]
    pieces = [(0, 1), (rt - 1, 1)] + [(a, b - a) for a, b in zip(middle, middle[1:])]
    nchunk = len(pieces)
    vmem = pl.BlockSpec(memory_space=pltpu.VMEM)
    dma = lambda *s: pltpu.SemaphoreType.DMA(s)
    return pl.pallas_call(
        functools.partial(main_kernel, nrow, ncol, tuple(pieces)),
        in_specs=[pl.BlockSpec(memory_space=pltpu.HBM)] + [vmem] * 7,
        out_specs=[vmem] * 3,
        out_shape=[
            pltpu.VMEM((rows, cols), F32),
            pltpu.VMEM((slots, cols), F32),
            pltpu.VMEM((2, slots, cols), F32),
        ],
        scratch_shapes=[
            pltpu.VMEM((5, ct, NGY), F32),
            pltpu.VMEM((5, NGY, table.shape[1]), F32),
            pltpu.VMEM((3, NGY, cols), F32),
            pltpu.VMEM((ct, NGY + 2 * PAD, NGY), F32),
            pltpu.VMEM((ct, NGY + 2 * PAD, NGY), F32),
            pltpu.VMEM((rows, NGY), F32),
            pltpu.VMEM((rows, NGY), F32),
            pltpu.VMEM((ct, NGY, NGY), F32),
            pltpu.VMEM((ct, NGY, NGY), F32),
            pltpu.VMEM((ct, NGY, NGY), F32),
            pltpu.VMEM((ct, NGY, NGY), F32),
            pltpu.VMEM((2, WMAX, cols), F32),
            pltpu.VMEM((3, own, NGY), F32),
            pltpu.VMEM((3, own, NGY), F32),
            pltpu.VMEM((nrow, WMAX, NGY), F32),
            pltpu.VMEM((slots, slots), F32),
            pltpu.VMEM((slots, NGY), F32),
            dma(3), dma(2, nchunk), dma(2, nchunk), dma(2), dma(2), dma(2, 3), dma(2, 3),
            dma(nrow), dma(nrow), dma(ncol), dma(ncol), dma(2, nrow), dma(nrow), dma(2), dma(2),
            dma(2, 2 * nrow), dma(2, 2 * nrow), dma(2, 2 * nrow), dma(2, 2 * nrow),
        ],
        compiler_params=pltpu.CompilerParams(
            collective_id=0, has_side_effects=True, vmem_limit_bytes=SCOPED
        ),
        name="main",
    )(cov, bp, sp, ownc, ownp, colc, diag, table)


def final_kernel(pred_ref, w_ref, strip_ref, o_ref, wide):
    i = pl.program_id(0)
    tile = o_ref.shape[0]
    cols = o_ref.shape[1]
    slots = w_ref.shape[0]

    @pl.when(i == 0)
    def _():
        hi = w_ref[...].astype(BF16)
        wide[:slots] = hi
        wide[slots : 2 * slots] = hi
        wide[2 * slots :] = (w_ref[...] - hi.astype(F32)).astype(BF16)

    part = cols // tile
    at = pl.ds(pl.multiple_of(lax.rem(i, part) * tile, tile), tile)
    s = strip_ref[i // part, :, at].T
    hi = s.astype(BF16)
    lo = (s - hi.astype(F32)).astype(BF16)
    s = jnp.concatenate([hi, lo, hi], axis=1)
    rat = pl.ds(pl.multiple_of(i * tile, tile), tile)
    for k in range(cols // 256):
        cat = slice(k * 256, (k + 1) * 256)
        o_ref[:, cat] = pred_ref[rat, cat] - jnp.dot(s, wide[:, cat], preferred_element_type=F32)


def final(pred, w, strip):
    rows, cols = pred.shape
    tile = 512
    vmem = pl.BlockSpec(memory_space=pltpu.VMEM)
    return pl.pallas_call(
        final_kernel,
        grid=(rows // tile,),
        in_specs=[vmem] * 3,
        out_specs=pl.BlockSpec((tile, cols), lambda i: (i, 0)),
        out_shape=jax.ShapeDtypeStruct((rows, cols), F32),
        scratch_shapes=[pltpu.VMEM((3 * w.shape[0], cols), BF16)],
        compiler_params=pltpu.CompilerParams(vmem_limit_bytes=SCOPED),
        name="final",
    )(keep(pred), keep(w), keep(strip))


def solution(mesh):
    nrow, ncol = mesh.shape["row"], mesh.shape["col"]

    def shards(covariance, center, links, process, wells, noise):
        center = center.reshape(-1, NGY)
        process = process.reshape(-1, NGY)
        small = prep(nrow, ncol, wells, noise, center, links, process, covariance)
        return final(*main(nrow, ncol, covariance, *small))

    in_specs = (P("row", "col"), P(), P(), P(), P(), P())
    out_specs = P("row", "col")
    return jax.shard_map(shards, mesh=mesh, in_specs=in_specs, out_specs=out_specs, check_vma=False)
```

```python
import functools

import jax
import jax.numpy as jnp
from jax import lax
from jax.experimental import pallas as pl
from jax.experimental.pallas import tpu as pltpu
from jax.sharding import PartitionSpec as P

NGY = 128
WMAX = 32
PANEL = 32
PAD = 8
RG = 16
SCOPED = 24 * 2**20
HIGHEST = lax.Precision.HIGHEST
F32 = jnp.float32
BF16 = jnp.bfloat16
MESH = pl.DeviceIdType.MESH


def iota(shape, dim):
    return lax.broadcasted_iota(jnp.int32, shape, dim).astype(F32)


def rowdot(a, b, precision=HIGHEST):
    return lax.dot_general(
        a, b, (((1,), (1,)), ((), ())), precision=precision, preferred_element_type=F32
    )


def coldot(a, b, precision=HIGHEST):
    return lax.dot_general(
        a, b, (((0,), (0,)), ((), ())), precision=precision, preferred_element_type=F32
    )


def prep_kernel(
    nrow, wells_hbm, noise_hbm, center_hbm, links_hbm, process_hbm, cov_ref,
    bp_ref, sp_ref, ownc_ref, ownp_ref, colc_ref, diag_ref, table_ref,
    wells_ref, noise_ref, center_ref, links_ref, process_ref, in_sem, tables, cells, rows_v, rows_s, coef, near, spill, idx_sem, near_sem, spill_sem,
):
    rows, cols = cov_ref.shape
    sources = (wells_hbm, noise_hbm, center_hbm, links_hbm, process_hbm)
    inputs = (wells_ref, noise_ref, center_ref, links_ref, process_ref)
    loads = [pltpu.make_async_copy(a, b, in_sem.at[n]) for n, (a, b) in enumerate(zip(sources, inputs))]
    for load in loads:
        load.start()
    for load in loads[:2]:
        load.wait()
    m = wells_ref.shape[1]
    slots = diag_ref.shape[0]
    ngx = center_ref.shape[0]
    own = bp_ref.shape[0]
    span = own + 2 * WMAX
    r = lax.axis_index("row")
    c = lax.axis_index("col")

    w = wells_ref[...].astype(F32)
    block = jnp.floor(w * (1.0 / cols))
    square = jnp.broadcast_to(block, (m, m)).T
    earlier = (square == block) & (iota((m, m), 0) < iota((m, m), 1))
    rank = jnp.sum(jnp.where(earlier, 1.0, 0.0), axis=0, keepdims=True)
    slot = block * WMAX + rank
    onehot = slot == iota((slots, m), 0)
    cell = jnp.sum(jnp.where(onehot, w + 1.0, 0.0), axis=1, keepdims=True) - 1.0
    noise = jnp.sum(jnp.where(onehot, noise_ref[...], 0.0), axis=1, keepdims=True)
    diag_ref[...] = jnp.broadcast_to(jnp.where(cell < 0.0, 1.0, noise), diag_ref.shape)
    cells[...] = jnp.full(cells.shape, -1.0, F32)
    cells[WMAX : WMAX + slots, :] = jnp.broadcast_to(cell, (slots, NGY))

    mine = cells[pl.ds(pl.multiple_of(r * own, WMAX), span), :]
    colc_ref[...] = cells[pl.ds(pl.multiple_of(WMAX + c * WMAX, WMAX), WMAX), :]
    ownc_ref[...] = mine[WMAX : WMAX + own]
    local = mine - (r * rows).astype(F32)
    rows_v[...] = local.T[0:8].astype(jnp.int32)
    copy = pltpu.make_async_copy(rows_v, rows_s, idx_sem)
    copy.start()

    for load in loads[2:]:
        load.wait()
    tables[:, 0:NGY] = center_ref[...]
    for g in range(ngx):
        for t in range(4):
            tables[g : g + 1, (t + 1) * NGY : (t + 2) * NGY] = links_ref[t : t + 1, g * NGY : (g + 1) * NGY]
    tables[:, 5 * NGY :] = process_ref[...]
    for t in range(6):
        table_ref[t] = tables[:, t * NGY : (t + 1) * NGY]
    gx = jnp.floor(mine[:, :1] * (1.0 / NGY))
    gy = mine[:, :1] - gx * NGY
    pickx = jnp.where(gx == iota((span, ngx), 1), 1.0, 0.0)
    table = jnp.dot(pickx, tables[...], precision=HIGHEST)
    copy.wait()

    moves = (0, -NGY, NGY, -1, 1)

    def row(i):
        return cov_ref.at[pl.ds(jnp.clip(i, 0, rows - 1), 1), :]

    def gather(i, carry):
        at = rows_s[0, WMAX + i]
        for t in range(5):
            dst = near.at[pl.ds(t * own + i, 1), :]
            pltpu.make_async_copy(row(at + moves[t]), dst, near_sem).start()
        return carry

    lax.fori_loop(0, own, gather, 0)

    def gather_spill(i, carry):
        low = spill.at[pl.ds(i, 1), :]
        high = spill.at[pl.ds(WMAX + i, 1), :]
        pltpu.make_async_copy(row(rows_s[0, i] + NGY), low, spill_sem).start()
        pltpu.make_async_copy(row(rows_s[0, WMAX + own + i] - NGY), high, spill_sem).start()
        return carry

    lax.fori_loop(0, WMAX, gather_spill, 0)

    picky = gy == iota((span, NGY), 1)
    valid = mine[:, :1] >= 0.0
    lv = local[:, :1]
    for t in range(5):
        value = jnp.sum(
            jnp.where(picky, table[:, t * NGY : (t + 1) * NGY], 0.0), axis=1, keepdims=True
        )
        target = lv + moves[t]
        ok = valid & (target >= 0.0) & (target < rows)
        if t == 3:
            ok = ok & (gy > 0.0)
        if t == 4:
            ok = ok & (gy < NGY - 1.0)
        coef[t] = jnp.broadcast_to(jnp.where(ok, value, 0.0), (span, NGY))
    value = jnp.sum(jnp.where(picky, table[:, 5 * NGY :], 0.0), axis=1, keepdims=True)
    value = jnp.where(valid, value, 0.0)
    ownp_ref[...] = jnp.broadcast_to(value[WMAX : WMAX + own], (own, NGY))

    pltpu.make_async_copy(cov_ref.at[pl.ds(0, 5 * own), :], near, near_sem).wait()
    pltpu.make_async_copy(cov_ref.at[pl.ds(0, 2 * WMAX), :], spill, spill_sem).wait()
    for k in range(cols // NGY):
        at = slice(k * NGY, (k + 1) * NGY)
        acc = coef[0, WMAX : WMAX + own] * near[0:own, at]
        for t in range(1, 5):
            acc = acc + coef[t, WMAX : WMAX + own] * near[t * own : (t + 1) * own, at]
        bp_ref[:, at] = acc
        sp_ref[:WMAX, at] = coef[2, :WMAX] * spill[:WMAX, at]
        sp_ref[WMAX:, at] = coef[1, WMAX + own :] * spill[WMAX:, at]


def keep(a):
    return pltpu.with_memory_space_constraint(a, pltpu.VMEM)


def prep(nrow, ncol, wells, noise, center, links, process, cov):
    rows, cols = cov.shape
    ratio = rows // cols
    own = ratio * WMAX
    slots = ncol * WMAX
    span = own + 2 * WMAX
    m = wells.shape[1]
    vmem = pl.BlockSpec(memory_space=pltpu.VMEM)
    out = lambda *s: pltpu.HBM(s, F32)
    return pl.pallas_call(
        functools.partial(prep_kernel, nrow),
        in_specs=[pl.BlockSpec(memory_space=pltpu.HBM)] * 6,
        out_specs=[vmem] * 7,
        out_shape=[
            out(own, cols), out(2 * WMAX, cols), out(own, NGY), out(own, NGY),
            out(WMAX, NGY), out(slots, NGY), out(6, center.shape[0], NGY),
        ],
        scratch_shapes=[
            pltpu.VMEM(wells.shape, jnp.int32),
            pltpu.VMEM(noise.shape, F32),
            pltpu.VMEM(center.shape, F32),
            pltpu.VMEM(links.shape, F32),
            pltpu.VMEM(process.shape, F32),
            pltpu.SemaphoreType.DMA((5,)),
            pltpu.VMEM((center.shape[0], 6 * NGY), F32),
            pltpu.VMEM((slots + 2 * WMAX, NGY), F32),
            pltpu.VMEM((8, span), jnp.int32),
            pltpu.SMEM((8, span), jnp.int32),
            pltpu.VMEM((5, span, NGY), F32),
            pltpu.VMEM((5 * own, cols), F32),
            pltpu.VMEM((2 * WMAX, cols), F32),
            pltpu.SemaphoreType.DMA,
            pltpu.SemaphoreType.DMA,
            pltpu.SemaphoreType.DMA,
        ],
        compiler_params=pltpu.CompilerParams(vmem_limit_bytes=SCOPED),
        name="prep",
    )(*[pltpu.with_memory_space_constraint(a, pltpu.HBM) for a in (wells, noise, center, links, process)], cov)


def eliminate(a_ref, dcol, first):
    slots = a_ref.shape[0]
    groups = PANEL // 8
    tiles = slots // NGY
    last = first + PANEL
    sub = lax.broadcasted_iota(jnp.int32, (8, NGY), 0)
    lane = lax.broadcasted_iota(jnp.int32, (8, NGY), 1)
    full = lambda v: jnp.broadcast_to(v, (8, NGY))
    rows = [slice(first + 8 * g, first + 8 * g + 8) for g in range(groups)]
    col, strip, dinv = {}, {}, {}
    for g in range(groups):
        for j in range(8 * g + 8):
            col[g, j] = full(a_ref[rows[g], first + j : first + j + 1])
        for t in range(tiles):
            at = lane + t * NGY
            inside = (at >= first) & (at < last)
            eye = jnp.where(at - first == sub + 8 * g, 1.0, 0.0)
            strip[g, t] = jnp.where(inside, eye, a_ref[rows[g], t * NGY : (t + 1) * NGY])
        dinv[g] = jnp.zeros((8, NGY), F32)
    for k in range(PANEL):
        gk, kk = divmod(k, 8)
        scale = 1.0 / full(col[gk, k][kk : kk + 1])
        dinv[gk] = jnp.where(sub == kk, scale, dinv[gk])
        low = {g: col[g, k] * scale for g in range(gk, groups)}
        low[gk] = jnp.where(sub > kk, low[gk], 0.0)
        for j in range(k + 1, PANEL):
            gj, jj = divmod(j, 8)
            up = full(col[gj, k][jj : jj + 1])
            for g in range(gj, groups):
                col[g, j] = col[g, j] - low[g] * up
        for t in range(tiles):
            row = full(strip[gk, t][kk : kk + 1])
            for g in range(gk, groups):
                strip[g, t] = strip[g, t] - low[g] * row
    u, x = [], []
    for g in range(groups):
        dcol[rows[g], :] = dinv[g]
        u.append(jnp.concatenate([strip[g, t] for t in range(tiles)], axis=1))
        x.append(
            jnp.concatenate(
                [jnp.where(lane + t * NGY >= last, strip[g, t] * dinv[g], 0.0) for t in range(tiles)], axis=1
            )
        )
    u = jnp.concatenate(u, axis=0)
    x = jnp.concatenate(x, axis=0)
    a_ref[first:last, :] = u
    if last < slots:
        base = last // NGY * NGY
        take = coldot(x[:, base:], u)
        at = lax.broadcasted_iota(jnp.int32, (slots - last, slots), 1)
        rest = jnp.where((at >= first) & (at < last), 0.0, a_ref[last:, :])
        a_ref[last:, :] = rest - take[last - base :]


def main_kernel(
    nrow, ncol, pieces,
    cov_ref, bp_ref, sp_ref, ownc_ref, ownp_ref, colc_ref, diag_ref,
    table_ref,
    pred_ref, across, strip_ref,
    ccol, rowt, xbuf, even, odd, lh, rh, rtop, rbot, rfirst, rlast,
    spin, hl, hr, gz, smat, dcol,
    x_sem, col_send, col_recv, spin_send, spin_recv, edge_send, edge_recv,
    gz_send, gz_recv, s_send, s_recv, ac_send, ac_recv, halo_send, halo_recv,
    ring_send, ring_recv, swap_send, swap_recv,
):
    rows, cols = cov_ref.shape
    rt = rows // NGY
    ct = cols // NGY
    own = bp_ref.shape[0]
    slots = across.shape[0]
    ngx = table_ref.shape[1]
    r = lax.axis_index("row")
    c = lax.axis_index("col")
    up, down = r > 0, r < nrow - 1
    lef, rig = c > 0, c < ncol - 1
    one = lambda cond: jnp.where(cond, 1, 0)

    def remote(src, dst, ssem, rsem, dr, dc):
        return pltpu.make_async_remote_copy(
            src_ref=src, dst_ref=dst, send_sem=ssem, recv_sem=rsem,
            device_id={"row": dr, "col": dc}, device_id_type=MESH,
        )

    base = pl.multiple_of(c * ct, 8)
    lane = lax.broadcasted_iota(jnp.int32, (ct, NGY), 1)
    for t in range(5):
        v = table_ref[t, pl.ds(base, ct), :]
        if t == 3:
            v = jnp.where(lane == 0, 0.0, v)
        if t == 4:
            v = jnp.where(lane == NGY - 1, 0.0, v)
        ccol[t] = v

    sub = lax.broadcasted_iota(jnp.int32, (NGY, ngx), 0)
    for t in range(5):
        v = table_ref[t].T
        if t == 3:
            v = jnp.where(sub == 0, 0.0, v)
        if t == 4:
            v = jnp.where(sub == NGY - 1, 0.0, v)
        rowt[t] = v

    even[...] = jnp.zeros(even.shape, F32)
    odd[...] = jnp.zeros(odd.shape, F32)

    @pl.when(r == 0)
    def _():
        rtop[...] = jnp.zeros(rtop.shape, F32)
        spin[0] = jnp.zeros(spin.shape[1:], F32)
        hl[1] = jnp.zeros(hl.shape[1:], F32)
        hr[1] = jnp.zeros(hr.shape[1:], F32)

    @pl.when(r == nrow - 1)
    def _():
        rbot[...] = jnp.zeros(rbot.shape, F32)
        spin[1] = jnp.zeros(spin.shape[1:], F32)
        hl[2] = jnp.zeros(hl.shape[1:], F32)
        hr[2] = jnp.zeros(hr.shape[1:], F32)

    @pl.when(c == 0)
    def _():
        lh[...] = jnp.zeros(lh.shape, F32)
        hl[...] = jnp.zeros(hl.shape, F32)

    @pl.when(c == ncol - 1)
    def _():
        rh[...] = jnp.zeros(rh.shape, F32)
        hr[...] = jnp.zeros(hr.shape, F32)

    bar = pltpu.get_barrier_semaphore()

    def greet(dr, dc):
        pl.semaphore_signal(bar, 1, device_id={"row": dr, "col": dc}, device_id_type=MESH)

    for d in range(1, nrow):
        greet(lax.rem(r + d, nrow), c)
    for d in range(1, ncol):
        greet(r, lax.rem(c + d, ncol))
    for dr, okr in ((-1, up), (1, down)):
        for dc, okc in ((-1, lef), (1, rig)):
            @pl.when(okr & okc)
            def _():
                greet(r + dr, c + dc)
    diagonals = (one(up) + one(down)) * (one(lef) + one(rig))
    pl.semaphore_wait(bar, nrow - 1 + ncol - 1 + diagonals)

    half_rows = lambda k: pl.ds(k * WMAX, WMAX)
    small = []

    def exchange(cond_send, cond_recv, src, dst, ssem, rsem, dr, dc):
        copy = remote(src, dst, ssem, rsem, dr, dc)
        pl.when(cond_send)(copy.start)
        small.append((cond_send, cond_recv, copy))

    exchange(up, down, sp_ref.at[half_rows(0)], spin.at[1], spin_send.at[0], spin_recv.at[0], r - 1, c)
    exchange(down, up, sp_ref.at[half_rows(1)], spin.at[0], spin_send.at[1], spin_recv.at[1], r + 1, c)
    for side, ok, no, buf, dc in ((0, lef, rig, hr, -1), (1, rig, lef, hl, 1)):
        at = slice(0, NGY) if side == 0 else slice(cols - NGY, cols)
        exchange(ok, no, bp_ref.at[:, at], buf.at[0], edge_send.at[side, 0], edge_recv.at[side, 0], r, c + dc)
        exchange(
            up & ok, down & no, sp_ref.at[half_rows(0), at], buf.at[2, half_rows(0)],
            edge_send.at[side, 1], edge_recv.at[side, 1], r - 1, c + dc,
        )
        exchange(
            down & ok, up & no, sp_ref.at[half_rows(1), at], buf.at[1, half_rows(0)],
            edge_send.at[side, 2], edge_recv.at[side, 2], r + 1, c + dc,
        )

    cols_out = []
    for n, (t0, tiles) in enumerate(pieces):
        at = pl.ds(t0 * NGY, tiles * NGY)
        to_left = remote(cov_ref.at[at, 0:NGY], rh.at[at], col_send.at[0, n], col_recv.at[0, n], r, c - 1)
        to_right = remote(
            cov_ref.at[at, cols - NGY : cols], lh.at[at], col_send.at[1, n], col_recv.at[1, n], r, c + 1
        )
        cols_out.append((to_left, to_right))

    def start_cols(n):
        if n < len(pieces):
            pl.when(lef)(cols_out[n][0].start)
            pl.when(rig)(cols_out[n][1].start)

    for n in range(3):
        start_cols(n)

    def fetch(t):
        b = lax.rem(t, 3)
        return pltpu.make_async_copy(
            cov_ref.at[pl.ds(pl.multiple_of(t * NGY, NGY), NGY), :], xbuf.at[b], x_sem.at[b]
        )

    fetch(0).start()
    fetch(1).start()

    groups = NGY // RG
    first = min(4, (rt - 2) // 4)
    second = min(8, (rt - 2) // 2)

    def right_group(t, b, g, k, before, here):
        at = pl.ds(pl.multiple_of(g * RG, RG), RG)
        gat = pl.ds(pl.multiple_of(t * NGY + g * RG, RG), RG)
        if k < 0:
            return lh[gat, :], xbuf[b, at, 0:NGY]
        after = xbuf[b, at, (k + 1) * NGY : (k + 2) * NGY] if k < ct - 1 else rh[gat, :]
        acc = ccol[0, k : k + 1] * here + ccol[1, k : k + 1] * before + ccol[2, k : k + 1] * after
        acc = acc + ccol[3, k : k + 1] * pltpu.roll(here, 1, 1)
        acc = acc + ccol[4, k : k + 1] * pltpu.roll(here, NGY - 1, 1)
        return here, after, acc

    def right_apply(t, b, dst, pad):
        def body(g, carry):
            before, here = right_group(t, b, g, -1, None, None)
            for k in range(ct):
                before, here, acc = right_group(t, b, g, k, before, here)
                dst[k, pl.ds(pl.multiple_of(pad + g * RG, 8), RG), :] = acc
            return carry

        lax.fori_loop(0, groups, body, 0)

    def left_apply(i, mid, other, following):
        gx = r * rt + i
        turn = lax.rem(ngx - gx, ngx)
        b = lax.rem(i + 1, 3)

        def body(g, carry):
            s = pl.ds(pl.multiple_of(g * RG, RG), RG)
            c0, c1, c2, c3, c4 = [
                jnp.broadcast_to(pltpu.roll(rowt[t, s], turn, 1)[:, 0:1], (RG, NGY)) for t in range(5)
            ]
            a0 = PAD + g * RG
            same = pl.ds(pl.multiple_of(a0, 8), RG)
            above = pl.ds(a0 - 1, RG)
            below = pl.ds(a0 + 1, RG)
            at = pl.ds(pl.multiple_of(i * NGY + g * RG, RG), RG)
            if following:
                before, here = right_group(i + 1, b, g, -1, None, None)
            for k in range(ct):
                acc = c0 * mid[k, same] + c1 * other[k, same]
                acc = acc + c3 * mid[k, above] + c4 * mid[k, below]
                if following:
                    before, here, nxt_row = right_group(i + 1, b, g, k, before, here)
                    other[k, same] = nxt_row
                    acc = acc + c2 * nxt_row
                pred_ref[at, k * NGY : (k + 1) * NGY] = acc
            return carry

        lax.fori_loop(0, groups, body, 0)

    def add_process(i):
        gx = r * rt + i
        kd = gx - c * ct

        @pl.when((kd >= 0) & (kd < ct))
        def _():
            sub = lax.broadcasted_iota(jnp.int32, (NGY, NGY), 0)
            lan = lax.broadcasted_iota(jnp.int32, (NGY, NGY), 1)
            add = jnp.where(sub == lan, table_ref[5, pl.ds(gx, 1), :], 0.0)
            rat = pl.ds(pl.multiple_of(i * NGY, NGY), NGY)
            cat = pl.ds(pl.multiple_of(kd * NGY, NGY), NGY)
            pred_ref[rat, cat] = pred_ref[rat, cat] + add

    def wait_cols(n):
        pl.when(rig)(cols_out[n][0].wait_recv)
        pl.when(lef)(cols_out[n][1].wait_recv)

    wait_cols(0)
    wait_cols(1)
    last = pltpu.make_async_copy(cov_ref.at[pl.ds(rows - NGY, NGY), :], xbuf.at[2], x_sem.at[2])
    last.start()
    fetch(0).wait()
    right_apply(0, 0, even, PAD)
    last.wait()
    right_apply(rt - 1, 2, rlast, 0)
    fetch(2).start()

    def save(k, carry):
        rfirst[k] = even[k, PAD : PAD + NGY, :]
        return carry

    lax.fori_loop(0, ct, save, 0)

    send_up = remote(rfirst, rbot, halo_send.at[0], halo_recv.at[0], r - 1, c)
    send_down = remote(
        rlast, rtop, halo_send.at[1], halo_recv.at[1], r + 1, c
    )

    reach = lambda i: jnp.minimum(i * (turns - 1) // (rt - 2), turns - 1)

    def take_turn(t, carry):
        relay(t)
        return carry

    def step(i, mid, other):
        for n in range(2, len(pieces)):
            @pl.when(i + 1 == pieces[n][0])
            def _():
                wait_cols(n)
                start_cols(n + 2)

        @pl.when(i == rt // 2)
        def _():
            pl.when(up)(send_up.start)
            pl.when(down)(send_down.start)

        done = jnp.where(i == 0, 1, reach(i - 1) + 1)
        lax.fori_loop(done, reach(i) + 1, take_turn, 0)
        fetch(i + 1).wait()

        @pl.when(i + 3 < rt)
        def _():
            fetch(i + 3).start()

        left_apply(i, mid, other, True)
        add_process(i)

    def pair(p, carry):
        step(2 * p, even, odd)
        step(2 * p + 1, odd, even)
        return carry

    for cond_send, cond_recv, copy in small:
        pl.when(cond_recv)(copy.wait_recv)

    mine = pl.ds(pl.multiple_of(r * own, own), own)

    def total(k):
        if k < 0:
            main, top, bottom = hl[0], hl[1, 0:WMAX], hl[2, 0:WMAX]
        elif k == ct:
            main, top, bottom = hr[0], hr[1, 0:WMAX], hr[2, 0:WMAX]
        else:
            at = slice(k * NGY, (k + 1) * NGY)
            main, top, bottom = bp_ref[:, at], spin[0, :, at], spin[1, :, at]
        if own == 2 * WMAX:
            return main + jnp.concatenate([top, bottom], axis=0)
        gap = jnp.zeros((own - 2 * WMAX, NGY), F32)
        return main + jnp.concatenate([top, gap, bottom], axis=0)

    cell_at = ownc_ref[...] - (c * cols).astype(F32)
    before, here = total(-1), total(0)
    for k in range(ct):
        after = total(k + 1)
        acc = ccol[0, k : k + 1] * here + ccol[1, k : k + 1] * before + ccol[2, k : k + 1] * after
        acc = acc + ccol[3, k : k + 1] * pltpu.roll(here, 1, 1)
        acc = acc + ccol[4, k : k + 1] * pltpu.roll(here, NGY - 1, 1)
        hit = cell_at == iota((own, NGY), 1) + k * NGY
        acc = acc + jnp.where(hit, ownp_ref[...], 0.0)
        across[mine, k * NGY : (k + 1) * NGY] = acc
        before, here = here, after

    nchip = ncol // 2
    hop = nchip // 2
    chip, core = c // 2, lax.rem(c, 2)

    def place(q):
        return jnp.where(lax.rem(q, 2) == 0, q // 2, nchip - 1 - q // 2)

    def chip_at(pos):
        pos = lax.rem(pos + nchip, nchip)
        return jnp.where(pos < hop, 2 * pos, 2 * (nchip - 1 - pos) + 1)

    pos, src_pos = place(chip), place(r)
    dist = (lax.rem(pos - src_pos + nchip, nchip), lax.rem(src_pos - pos + nchip, nchip))
    nxt = (chip_at(pos + 1) * 2 + core, chip_at(pos - 1) * 2 + core)
    is_src = dist[0] == 0
    count = 2 * nrow
    turns = count + nchip - 1
    share = (own // 4 // 2, own * 3 // 4 // 2)

    def nearest(n):
        table = [sorted(range(nrow), key=lambda z: abs(z - q)) for q in range(nrow)]
        z = 0
        for q in range(nrow):
            for m in range(nrow):
                z = z + jnp.where((r == q) & (n == m), table[q][m], 0)
        return z

    def pass_on(src, dst):
        at = pl.ds(pl.multiple_of(src * own, own), own)
        side = jnp.where(dst > r, 1, 0)
        return remote(across.at[at], across.at[at], ac_send.at[side, src], ac_recv.at[src], dst, c)

    def gather_turn(u):
        @pl.when(r - u >= 0)
        def _():
            copy = pass_on(r - u, r + 1)
            copy.wait_recv()
            pl.when(down)(copy.start)

        @pl.when(r + u < nrow)
        def _():
            copy = pass_on(r + u, r - 1)
            copy.wait_recv()
            pl.when(up)(copy.start)

    def gather_drain():
        for u in range(nrow - 1):
            @pl.when((r - u >= 0) & down)
            def _():
                pass_on(r - u, r + 1).wait_send()

            @pl.when((r + u < nrow) & up)
            def _():
                pass_on(r + u, r - 1).wait_send()

    def moves(n, h):
        z = nearest(n // 2)
        start = z * own + h * 2 * share[0] + lax.rem(n, 2) * share[h]
        at = pl.ds(pl.multiple_of(start, 8), share[h])
        here, there = strip_ref.at[core, at], strip_ref.at[1 - core, at]
        fwd = remote(here, here, ring_send.at[h, n], ring_recv.at[h, n], r, nxt[h])
        swap = remote(here, here, swap_send.at[h, n], swap_recv.at[h, n], r, c + 1 - 2 * core)
        back = remote(there, there, swap_send.at[h, n], swap_recv.at[h, n], r, c + 1 - 2 * core)
        return at, fwd, swap, back

    def relay(t):
        @pl.when((lax.rem(t, 2) == 0) & (t >= 2) & (t < count))
        def _():
            gather_turn(t // 2)

        for h in range(2):
            n = t - dist[h]

            @pl.when((n >= 0) & (n < count))
            def _():
                at, fwd, swap, _ = moves(n, h)

                @pl.when(is_src)
                def _():
                    strip_ref[core, at, :] = across[at, :]

                @pl.when(jnp.logical_not(is_src))
                def _():
                    fwd.wait_recv()

                pl.when(dist[h] < nchip - 1)(fwd.start)
                swap.start()

    pl.when(down)(pass_on(r, r + 1).start)
    pl.when(up)(pass_on(r, r - 1).start)
    relay(0)
    start_cols(3)

    pick_at = colc_ref[...] - (c * cols).astype(F32)
    pick = jnp.where(pick_at[:, 0:1] == iota((WMAX, cols), 1), 1.0, 0.0)
    gram = rowdot(pick, across[mine, :])
    gz[r, :, 0:own] = gram

    gz_out = []
    for d in range(1, nrow):
        peer = lax.rem(r + d, nrow)
        copy = remote(gz.at[r], gz.at[r], gz_send.at[d - 1], gz_recv.at[r], peer, c)
        copy.start()
        gz_out.append(copy)
    lax.fori_loop(0, first, pair, 0)
    for d in range(1, nrow):
        src = lax.rem(r + d, nrow)
        remote(gz.at[src], gz.at[src], gz_send.at[0], gz_recv.at[src], src, c).wait_recv()
    srow = pl.ds(pl.multiple_of(c * WMAX, WMAX), WMAX)
    for j in range(nrow):
        smat[srow, j * own : (j + 1) * own] = gz[j, :, 0:own]
    s_out = []
    for d in range(1, ncol):
        peer = lax.rem(c + d, ncol)
        copy = remote(smat.at[srow], smat.at[srow], s_send.at[d - 1], s_recv.at[c], r, peer)
        copy.start()
        s_out.append(copy)
    lax.fori_loop(first, second, pair, 0)
    for d in range(1, ncol):
        src = lax.rem(c + d, ncol)
        at = pl.ds(pl.multiple_of(src * WMAX, WMAX), WMAX)
        remote(smat.at[at], smat.at[at], s_send.at[0], s_recv.at[src], r, src).wait_recv()


    for copy in s_out:
        copy.wait_send()

    tiles = [slice(k * NGY, (k + 1) * NGY) for k in range(slots // NGY)]
    for at in tiles:
        eye = lax.broadcasted_iota(jnp.int32, (slots, NGY), 0) == (
            lax.broadcasted_iota(jnp.int32, (slots, NGY), 1) + at.start
        )
        smat[:, at] = smat[:, at] + jnp.where(eye, diag_ref[...], 0.0)
    for top in range(0, slots, PANEL):
        eliminate(smat, dcol, top)

    lax.fori_loop(second, (rt - 2) // 2, pair, 0)
    step(rt - 2, even, odd)
    left_apply(rt - 1, odd, even, False)
    add_process(rt - 1)

    gather_drain()
    at = lax.broadcasted_iota(jnp.int32, (slots, slots), 1)
    low = jnp.where(at <= lax.broadcasted_iota(jnp.int32, (slots, slots), 0), smat[...], 0.0)
    inverse = coldot(low, low * dcol[:, 0:1])
    wt = cols // 2 if cols // 2 % NGY == 0 else cols
    for k in range(cols // wt):
        at = slice(k * wt, (k + 1) * wt)
        across[:, at] = jnp.dot(inverse, across[:, at], precision=HIGHEST)

    pl.when(down)(send_up.wait_recv)
    pl.when(up)(send_down.wait_recv)
    for side, buf, link, t in ((0, rtop, 0, 0), (1, rbot, 1, rt - 1)):
        gx = r * rt + t
        v = jnp.broadcast_to(table_ref[1 + link, pl.ds(gx, 1), :], (NGY, NGY)).T
        for k in range(ct):
            rat = slice(t * NGY, (t + 1) * NGY)
            cat = slice(k * NGY, (k + 1) * NGY)
            pred_ref[rat, cat] = pred_ref[rat, cat] + v * buf[k]

    def drain(n, carry):
        for h in range(2):
            _, fwd, swap, back = moves(n, h)
            back.wait_recv()
            swap.wait_send()
            pl.when(dist[h] < nchip - 1)(fwd.wait_send)
        return carry

    lax.fori_loop(0, count, drain, 0)
    for copy in gz_out:
        copy.wait_send()
    for cond_send, cond_recv, copy in small:
        pl.when(cond_send)(copy.wait_send)
    for to_left, to_right in cols_out:
        pl.when(lef)(to_left.wait_send)
        pl.when(rig)(to_right.wait_send)
    pl.when(up)(send_up.wait_send)
    pl.when(down)(send_down.wait_send)


def main(nrow, ncol, cov, bp, sp, ownc, ownp, colc, diag, table):
    rows, cols = cov.shape
    rt, ct = rows // NGY, cols // NGY
    own = bp.shape[0]
    slots = diag.shape[0]
    middle = list(range(1, rt - 1, 5)) + [rt - 1]
    pieces = [(0, 1), (rt - 1, 1)] + [(a, b - a) for a, b in zip(middle, middle[1:])]
    nchunk = len(pieces)
    vmem = pl.BlockSpec(memory_space=pltpu.VMEM)
    dma = lambda *s: pltpu.SemaphoreType.DMA(s)
    return pl.pallas_call(
        functools.partial(main_kernel, nrow, ncol, tuple(pieces)),
        in_specs=[pl.BlockSpec(memory_space=pltpu.HBM)] + [vmem] * 7,
        out_specs=[vmem] * 3,
        out_shape=[
            pltpu.VMEM((rows, cols), F32),
            pltpu.VMEM((slots, cols), F32),
            pltpu.VMEM((2, slots, cols), F32),
        ],
        scratch_shapes=[
            pltpu.VMEM((5, ct, NGY), F32),
            pltpu.VMEM((5, NGY, table.shape[1]), F32),
            pltpu.VMEM((3, NGY, cols), F32),
            pltpu.VMEM((ct, NGY + 2 * PAD, NGY), F32),
            pltpu.VMEM((ct, NGY + 2 * PAD, NGY), F32),
            pltpu.VMEM((rows, NGY), F32),
            pltpu.VMEM((rows, NGY), F32),
            pltpu.VMEM((ct, NGY, NGY), F32),
            pltpu.VMEM((ct, NGY, NGY), F32),
            pltpu.VMEM((ct, NGY, NGY), F32),
            pltpu.VMEM((ct, NGY, NGY), F32),
            pltpu.VMEM((2, WMAX, cols), F32),
            pltpu.VMEM((3, own, NGY), F32),
            pltpu.VMEM((3, own, NGY), F32),
            pltpu.VMEM((nrow, WMAX, NGY), F32),
            pltpu.VMEM((slots, slots), F32),
            pltpu.VMEM((slots, NGY), F32),
            dma(3), dma(2, nchunk), dma(2, nchunk), dma(2), dma(2), dma(2, 3), dma(2, 3),
            dma(nrow), dma(nrow), dma(ncol), dma(ncol), dma(2, nrow), dma(nrow), dma(2), dma(2),
            dma(2, 2 * nrow), dma(2, 2 * nrow), dma(2, 2 * nrow), dma(2, 2 * nrow),
        ],
        compiler_params=pltpu.CompilerParams(
            collective_id=0, has_side_effects=True, vmem_limit_bytes=SCOPED
        ),
        name="main",
    )(cov, bp, sp, ownc, ownp, colc, diag, table)


def final_kernel(pred_ref, w_ref, strip_ref, o_ref, wide):
    i = pl.program_id(0)
    tile = o_ref.shape[0]
    cols = o_ref.shape[1]
    slots = w_ref.shape[0]

    @pl.when(i == 0)
    def _():
        hi = w_ref[...].astype(BF16)
        wide[:slots] = hi
        wide[slots : 2 * slots] = hi
        wide[2 * slots :] = (w_ref[...] - hi.astype(F32)).astype(BF16)

    part = cols // tile
    at = pl.ds(pl.multiple_of(lax.rem(i, part) * tile, tile), tile)
    s = strip_ref[i // part, :, at].T
    hi = s.astype(BF16)
    lo = (s - hi.astype(F32)).astype(BF16)
    s = jnp.concatenate([hi, lo, hi], axis=1)
    rat = pl.ds(pl.multiple_of(i * tile, tile), tile)
    for k in range(cols // 256):
        cat = slice(k * 256, (k + 1) * 256)
        o_ref[:, cat] = pred_ref[rat, cat] - jnp.dot(s, wide[:, cat], preferred_element_type=F32)


def final(pred, w, strip):
    rows, cols = pred.shape
    tile = 512
    vmem = pl.BlockSpec(memory_space=pltpu.VMEM)
    return pl.pallas_call(
        final_kernel,
        grid=(rows // tile,),
        in_specs=[vmem] * 3,
        out_specs=pl.BlockSpec((tile, cols), lambda i: (i, 0)),
        out_shape=jax.ShapeDtypeStruct((rows, cols), F32),
        scratch_shapes=[pltpu.VMEM((3 * w.shape[0], cols), BF16)],
        compiler_params=pltpu.CompilerParams(vmem_limit_bytes=SCOPED),
        name="final",
    )(keep(pred), keep(w), keep(strip))


def solution(mesh):
    nrow, ncol = mesh.shape["row"], mesh.shape["col"]

    def shards(covariance, center, links, process, wells, noise):
        center = center.reshape(-1, NGY)
        process = process.reshape(-1, NGY)
        small = prep(nrow, ncol, wells, noise, center, links, process, covariance)
        return final(*main(nrow, ncol, covariance, *small))

    in_specs = (P("row", "col"), P(), P(), P(), P(), P())
    out_specs = P("row", "col")
    return jax.shard_map(shards, mesh=mesh, in_specs=in_specs, out_specs=out_specs, check_vma=False)
```
